32 devices in a mesh: region: 8 (over z, y), strip: 4 (over x, core).
Axes of the slice: x: 2, y: 2, z: 4, core: 2. Of those that a mesh axis runs over, the one named last changes fastest.
Arguments:
- features: bfloat16 [32, 64, 32, 128], P(None, 'region', 'strip'), may hold values from -28 to 28
- brick_mask: int32 [8, 4, 16], P('region', 'strip'), may hold values from 0 to 1, as said below
- conv_first: bfloat16 [3, 3, 3, 32, 32], replicated, may hold values from -0.21875 to 0.21875
- conv_second: bfloat16 [3, 3, 3, 32, 32], replicated, may hold values from -0.21875 to 0.21875
- gain_first: float32 [32], replicated, may hold values from 0.5 to 1.5
- shift_first: float32 [32], replicated, may hold values from -2 to 2
- gain_second: float32 [32], replicated, may hold values from 0.5 to 1.5
- shift_second: float32 [32], replicated, may hold values from -2 to 2
Outputs:
- block_out: bfloat16 [32, 64, 32, 128], P(None, 'region', 'strip')
The draws below stay inside these ranges and needn't reach their ends.
Inputs may be any that keep to these rules, and one draw needn't show every extreme that they name: `brick_mask`: every device's block of 1 x 1 x 16 bricks holds at least one active brick.
All inputs are finite; a program needn't handle non-finite values.
Results may differ from the reference program's by a relative error of at most 0.0085.
Values may be sent and summed in bfloat16 or wider, within the bound.
No kernel may reach another device: no remote copies, remote signals or barrier semaphores. Data moves between devices by JAX's collectives and lax.ppermute only.
A program may use at most 64 MiB of HBM per device.

```python
import math
import jax
import jax.numpy as jnp
from jax import lax

C = 32
BRICK = 8
BXD = 1
BYD = 1
BZ = 16
NZ = 128
NXB = 8
NYB = 4
NX = 64
NY = 32


def smooth_field(key):
    field = jnp.clip(jax.random.normal(key, (NX, NY, NZ), jnp.float32), -3.0, 3.0)
    for direction in range(3):
        margins = [(0, 0), (0, 0), (0, 0)]
        margins[direction] = (2, 2)
        padded = jnp.pad(field, margins)
        extent = field.shape[direction]
        running = jnp.zeros_like(field)
        for displacement in range(5):
            running = running + lax.slice_in_dim(padded, displacement, displacement + extent, axis=direction)
        field = running / math.sqrt(5.0)
    return jnp.clip(field, -3.0, 3.0)


def draw_features(key, part):
    rough = jnp.clip(jax.random.normal(jax.random.fold_in(key, 11), (C, NX, NY, NZ), jnp.float32), -3.0, 3.0)
    common = smooth_field(jax.random.fold_in(key, 12))[None]
    place_x = lax.broadcasted_iota(jnp.float32, (1, NX, 1, 1), 1) / max(NX - 1, 1)
    place_y = lax.broadcasted_iota(jnp.float32, (1, 1, NY, 1), 2) / max(NY - 1, 1)
    channel_offset = jnp.clip(jax.random.normal(jax.random.fold_in(key, 14), (C, 1, 1, 1), jnp.float32), -1.0, 1.0)
    mixing = 0.15 + 0.7 * place_x
    amplitude = (0.5 + place_x) * (0.5 + 1.5 * place_y)
    noise = jnp.sqrt(1.0 - mixing * mixing) * rough + mixing * common
    return (noise * amplitude + channel_offset * amplitude).astype(jnp.bfloat16)


def draw_brick_mask(key, part):
    place_x = lax.broadcasted_iota(jnp.int32, (NXB, NYB, BZ), 0)
    place_y = lax.broadcasted_iota(jnp.int32, (NXB, NYB, BZ), 1)
    threshold = 150 + 450 * place_x // max(NXB - 1, 1) + 300 * place_y // max(NYB - 1, 1)
    rolls = jax.random.randint(jax.random.fold_in(key, 21), (NXB, NYB, BZ), 0, 1000)
    active = (rolls < threshold).astype(jnp.int32)
    blocks_x = NXB // BXD
    blocks_y = NYB // BYD
    chosen = jax.random.randint(jax.random.fold_in(key, 22), (blocks_x, 1, blocks_y, 1, 1), 0, BXD * BYD * BZ)
    inner_x = lax.broadcasted_iota(jnp.int32, (1, BXD, 1, BYD, BZ), 1)
    inner_y = lax.broadcasted_iota(jnp.int32, (1, BXD, 1, BYD, BZ), 3)
    inner_z = lax.broadcasted_iota(jnp.int32, (1, BXD, 1, BYD, BZ), 4)
    position = (inner_x * BYD + inner_y) * BZ + inner_z
    forced = (position == chosen).astype(jnp.int32).reshape(NXB, NYB, BZ)
    return jnp.maximum(active, forced)


def bell_draw(own_key, shape, scale, most, kind=jnp.bfloat16):
    values = scale * jax.random.normal(own_key, shape, jnp.float32)
    return jnp.clip(values, min=-most, max=most).astype(kind)


def setup_inputs(seed: int = 0) -> dict:
    keys = jax.random.split(jax.random.key(seed), 9)
    return {
        "features": draw_features(jax.random.fold_in(keys[8], 71), 0),
        "brick_mask": draw_brick_mask(jax.random.fold_in(keys[8], 71), 0),
        "conv_first": bell_draw(keys[2], (3, 3, 3, C, C), (27 * C) ** -0.5, 0.21875),
        "conv_second": bell_draw(keys[3], (3, 3, 3, C, C), (27 * C) ** -0.5, 0.21875),
        "gain_first": jnp.clip(1.0 + 0.1 * jax.random.normal(keys[4], (C,), jnp.float32), 0.5, 1.5),
        "shift_first": bell_draw(keys[5], (C,), 0.5, 2.0, jnp.float32),
        "gain_second": jnp.clip(1.0 + 0.1 * jax.random.normal(keys[6], (C,), jnp.float32), 0.5, 1.5),
        "shift_second": bell_draw(keys[7], (C,), 0.5, 2.0, jnp.float32),
    }


EPSILON = 1e-05

def expand(bricks):
    count_x, count_y, count_z = bricks.shape
    values = bricks.astype(jnp.float32)
    grown = jnp.broadcast_to(values[:, None, :, None, :, None], (count_x, BRICK, count_y, BRICK, count_z, BRICK))
    return grown.reshape(count_x * BRICK, count_y * BRICK, count_z * BRICK)

def convolve_grid(field, weight, voxel_mask):
    padded = jnp.pad(field, ((0, 0), (1, 1), (1, 1), (1, 1)))
    slab_width = BRICK * BXD
    blocks_total = NX // slab_width

    def slab_conv(block_index):
        offset = (block_index * slab_width).astype(jnp.int32)
        window_in = lax.dynamic_slice_in_dim(padded, offset, slab_width + 2, 1).astype(jnp.float32)
        running = jnp.zeros((C, slab_width, NY, NZ), jnp.float32)
        for step_x in range(3):
            for step_y in range(3):
                for step_z in range(3):
                    kernel = weight[step_x, step_y, step_z].astype(jnp.float32)
                    part_in = window_in[:, step_x:step_x + slab_width, step_y:step_y + NY, step_z:step_z + NZ]
                    running = running + jnp.einsum('io,ixyz->oxyz', kernel, part_in, precision=lax.Precision.HIGHEST)
        slab_mask = lax.dynamic_slice_in_dim(voxel_mask, offset, slab_width, 0)
        return (running * slab_mask).astype(jnp.bfloat16)
    stacked = lax.map(slab_conv, jnp.arange(blocks_total, dtype=jnp.int32))
    return stacked.transpose(1, 0, 2, 3, 4).reshape(C, NX, NY, NZ)

def moments(field, voxel_mask):
    active_total = jnp.sum(voxel_mask)

    def channel_stats(plane):
        values = plane.astype(jnp.float32)
        average = jnp.sum(values * voxel_mask) / active_total
        centered = (values - average) * voxel_mask
        return (average, jnp.sum(centered * centered) / active_total)
    return lax.map(channel_stats, field)

def normalized(field, voxel_mask, gain, shift, residual):
    average, variance = moments(field, voxel_mask)
    scale = lax.rsqrt(variance + EPSILON) * gain

    def channel_out(items):
        plane, mean_c, scale_c, shift_c, extra = items
        values = (plane.astype(jnp.float32) - mean_c) * scale_c + shift_c + extra.astype(jnp.float32)
        return (jax.nn.relu(values) * voxel_mask).astype(jnp.bfloat16)
    return lax.map(channel_out, (field, average, scale, shift, residual))

def reference(features, brick_mask, conv_first, conv_second, gain_first, shift_first, gain_second, shift_second):
    voxel_mask = expand(brick_mask)
    masked_input = features * voxel_mask.astype(jnp.bfloat16)
    first_out = convolve_grid(masked_input, conv_first, voxel_mask)
    activation = normalized(first_out, voxel_mask, gain_first, shift_first, jnp.zeros_like(first_out))
    second_out = convolve_grid(activation, conv_second, voxel_mask)
    return normalized(second_out, voxel_mask, gain_second, shift_second, masked_input)
```

```python
import jax
import jax.numpy as jnp
from jax import lax
from jax.sharding import PartitionSpec as P

BRICK = 8


EPSILON = 1e-05


def with_halo(block, sides, width):
    for axis, dim in sides:
        count = lax.axis_size(axis)
        forward = [(i, i + 1) for i in range(count - 1)]
        backward = [(target, source) for source, target in forward]
        low = lax.ppermute(
            lax.slice_in_dim(block, block.shape[dim] - width, None, axis=dim), axis, forward
        )
        high = lax.ppermute(lax.slice_in_dim(block, 0, width, axis=dim), axis, backward)
        block = jnp.concatenate([low, block, high], axis=dim)
    return block


def expand(bricks):
    count_x, count_y, count_z = bricks.shape
    values = bricks.astype(jnp.float32)
    grown = jnp.broadcast_to(
        values[:, None, :, None, :, None], (count_x, BRICK, count_y, BRICK, count_z, BRICK)
    )
    return grown.reshape(count_x * BRICK, count_y * BRICK, count_z * BRICK)


def convolve(padded, weight, extent_x, extent_y):
    depth = padded.shape[3]
    channels = padded.shape[0]
    framed = jnp.pad(padded, ((0, 0), (0, 0), (0, 0), (1, 1)))
    flat_kernel = weight.reshape(27 * channels, weight.shape[4])
    pieces = []
    for start in range(0, extent_x, 2):
        width = min(2, extent_x - start)
        windows = []
        for step_x in range(3):
            for step_y in range(3):
                for step_z in range(3):
                    windows.append(
                        framed[
                            :,
                            start + step_x : start + step_x + width,
                            step_y : step_y + extent_y,
                            step_z : step_z + depth,
                        ]
                    )
        stacked = jnp.concatenate(windows, axis=0)
        pieces.append(
            jnp.einsum("ko,kxyz->oxyz", flat_kernel, stacked, preferred_element_type=jnp.float32)
        )
    return jnp.concatenate(pieces, axis=1)


def exchange_sums(part):
    axes = ("region", "strip")
    count = lax.axis_size(axes)
    copies = jnp.broadcast_to(part[None, :], (count, part.shape[0]))
    return jnp.sum(lax.all_to_all(copies, axes, 0, 0, tiled=True), axis=0)


def moments(values, voxel_mask):
    channels = values.shape[0]
    part = jnp.concatenate(
        [
            jnp.sum(values * voxel_mask, axis=(1, 2, 3)),
            jnp.sum(values * values * voxel_mask, axis=(1, 2, 3)),
            jnp.sum(voxel_mask)[None],
            jnp.zeros((127 - 2 * channels % 128,), jnp.float32),
        ]
    )
    total = exchange_sums(part)
    active_total = total[2 * channels]
    average = total[:channels] / active_total
    variance = total[channels : 2 * channels] / active_total - average * average
    return (average, variance)


def normalize(values, average, variance, gain, shift):
    scale = lax.rsqrt(variance + EPSILON) * gain
    return (values - average[:, None, None, None]) * scale[:, None, None, None] + shift[
        :, None, None, None
    ]


def per_device(
    features,
    brick_mask,
    conv_first,
    conv_second,
    gain_first,
    shift_first,
    gain_second,
    shift_second,
):
    voxel_mask = expand(brick_mask)
    masked_input = features * voxel_mask.astype(jnp.bfloat16)
    channels, extent_x, extent_y, depth = features.shape
    padded = with_halo(masked_input, (("region", 1), ("strip", 2)), 1)
    first_out = (convolve(padded, conv_first, extent_x, extent_y) * voxel_mask).astype(jnp.bfloat16)
    first_values = first_out.astype(jnp.float32)
    average, variance = moments(first_values, voxel_mask)
    activation = (
        jax.nn.relu(normalize(first_values, average, variance, gain_first, shift_first))
        * voxel_mask
    ).astype(jnp.bfloat16)
    second_in = with_halo(activation, (("region", 1), ("strip", 2)), 1)
    second_out = (convolve(second_in, conv_second, extent_x, extent_y) * voxel_mask).astype(
        jnp.bfloat16
    )
    second_values = second_out.astype(jnp.float32)
    average, variance = moments(second_values, voxel_mask)
    result = (
        jax.nn.relu(
            normalize(second_values, average, variance, gain_second, shift_second)
            + masked_input.astype(jnp.float32)
        )
        * voxel_mask
    )
    return result.astype(jnp.bfloat16)


def solution(mesh):
    in_specs = (
        P(None, "region", "strip", None),
        P("region", "strip", None),
        P(),
        P(),
        P(),
        P(),
        P(),
        P(),
    )
    out_specs = P(None, "region", "strip", None)
    return jax.shard_map(
        per_device, mesh=mesh, in_specs=in_specs, out_specs=out_specs, check_vma=False
    )
```

```python
import functools

import jax
import jax.numpy as jnp
from jax import lax
from jax.experimental import pallas as pl
from jax.experimental.pallas import tpu as pltpu
from jax.sharding import PartitionSpec as P

BRICK = 8
EPSILON = 1e-05
HALO = 2
AXES = ("region", "strip")
F32 = jnp.float32
BF16 = jnp.bfloat16


def even_pairs(count):
    return [(i, i ^ 1) for i in range(count) if (i ^ 1) < count]


def odd_pairs(count):
    pairs = [(i, i + 1) for i in range(1, count - 1, 2)]
    return pairs + [(b, a) for a, b in pairs]


def swap(even, odd, axis):
    count = lax.axis_size(axis)
    return lax.ppermute(even, axis, even_pairs(count)), lax.ppermute(odd, axis, odd_pairs(count))


def whole(*_):
    return pl.BlockSpec(memory_space=pltpu.VMEM)


def call(body, outs, ins, scratch=(), flops=0, smem=0):
    in_specs = [pl.BlockSpec(memory_space=pltpu.SMEM)] * smem + [whole()] * (len(ins) - smem)
    return pl.pallas_call(
        body,
        out_shape=outs,
        in_specs=in_specs,
        out_specs=jax.tree.map(whole, outs),
        scratch_shapes=list(scratch),
        cost_estimate=pl.CostEstimate(
            flops=flops,
            transcendentals=0,
            bytes_accessed=sum(a.size * a.dtype.itemsize for a in ins),
        ),
    )(*ins)


def brick_rows(bricks, depth):
    count = bricks.shape[1]
    at = lax.broadcasted_iota(jnp.int32, (count, depth), 0)
    voxel = lax.broadcasted_iota(jnp.int32, (count, depth), 1)
    spread = (voxel // BRICK == at).astype(F32)
    return jnp.dot(bricks, spread, preferred_element_type=F32, precision=lax.Precision.HIGHEST)


def gather_kernel(dims, place, features, bricks, own, masks, even, odd, turned):
    channels, extent_x, extent_y, depth, bx, by = dims
    rows = brick_rows(bricks[...].astype(F32), depth)
    for i in range(bx * by):
        masks[i] = jnp.broadcast_to(rows[i : i + 1], (16, depth))
    for x in range(extent_x):
        for j in range(by):
            part = features[:, x, j * BRICK : (j + 1) * BRICK, :].astype(F32)
            part = part * masks[x // BRICK * by + j][None, :BRICK, :]
            turned[...] = part.reshape(channels * BRICK, depth)
            for y in range(BRICK):
                own[x, j * BRICK + y] = turned[pl.ds(y, channels, stride=BRICK), :].astype(BF16)
    first = place[0] == 0
    for out, low in ((even, jnp.where(first, 0, 1)), (odd, jnp.where(first, 1, 0))):
        start = jnp.where(low == 1, 0, extent_x - HALO)
        for i in range(HALO):
            for y in range(extent_y):
                at = (i * extent_y + y) * channels
                out[at : at + channels, :] = own[start + i, y]
        base = HALO * extent_y * channels
        for j in range(by):
            tile = masks[jnp.where(low == 1, 0, bx - 1) * by + j]
            out[base + 16 * j : base + 16 * (j + 1), :] = tile.astype(BF16)


def corner_kernel(dims, place, own, masks, from_even, from_odd, even, odd):
    channels, extent_x, extent_y, depth, bx, by = dims
    first_x = place[0] == 0
    first_y = place[1] == 0
    wide = extent_x + 2 * HALO
    base = HALO * extent_y * channels
    for out, low in ((even, jnp.where(first_y, 0, 1)), (odd, jnp.where(first_y, 1, 0))):
        start = jnp.where(low == 1, 0, extent_y - HALO)
        brick = jnp.where(low == 1, 0, by - 1)

        def put(x, j, value):
            at = (x * HALO + j) * channels
            out[at : at + channels, :] = value

        def put_mask(x, value):
            at = wide * HALO * channels + 16 * x
            out[at : at + 16, :] = value

        for x in range(extent_x):
            for j in range(HALO):
                put(HALO + x, j, own[x, start + j])
        for x in range(bx):
            put_mask(1 + x, masks[x * by + brick].astype(BF16))
        for i in range(HALO):
            for j in range(HALO):
                at = pl.multiple_of((i * extent_y + start + j) * channels, channels)
                a = from_even[pl.ds(at, channels), :]
                b = from_odd[pl.ds(at, channels), :]
                put(i, j, jnp.where(first_x, b, a))
                put(HALO + extent_x + i, j, jnp.where(first_x, a, b))
        at = pl.multiple_of(base + brick * 16, 16)
        a = from_even[pl.ds(at, 16), :]
        b = from_odd[pl.ds(at, 16), :]
        put_mask(0, jnp.where(first_x, b, a))
        put_mask(1 + bx, jnp.where(first_x, a, b))


def put_shifted(field, x, y, value):
    channels, depth = value.shape
    lane = lax.broadcasted_iota(jnp.int32, value.shape, 1)
    before = jnp.where(lane == 0, 0.0, pltpu.roll(value, 1, 1))
    after = jnp.where(lane == depth - 1, 0.0, pltpu.roll(value, depth - 1, 1))
    for k, part in enumerate((before, value, after)):
        at = (3 * y + k) * channels
        field[at : at + channels, x * depth : (x + 1) * depth] = part.astype(BF16)


def send_stats(out, channels, sums, squares, counts):
    depth = sums.shape[1]
    rest = jnp.zeros((128 - 2 * channels - counts.shape[0], depth), F32)
    table = jnp.concatenate([sums, squares, counts, rest], axis=0)
    row = jnp.sum(jnp.transpose(table), axis=0, keepdims=True)
    out[...] = jnp.broadcast_to(row, out.shape)


def affine(stats, gain, channels, depth):
    row = jnp.sum(stats[...], axis=0, keepdims=True)
    table = jnp.transpose(jnp.broadcast_to(row, (128, 128)))
    total = jnp.sum(table[2 * channels : 2 * channels + BRICK], axis=0, keepdims=True)
    average = table[:channels] / total
    variance = table[channels : 2 * channels] / total - average * average
    return average, lax.rsqrt(variance + EPSILON) * gain


def first_kernel(
    dims, place, own, masks, x_even, x_odd, y_even, y_odd, band, first_out, wide_masks, stats, field
):
    channels, extent_x, extent_y, depth, bx, by = dims
    first_x = place[0] == 0
    first_y = place[1] == 0
    wide_x = extent_x + 2 * HALO
    for x in range(extent_x):
        for y in range(extent_y):
            put_shifted(field, HALO + x, HALO + y, own[x, y].astype(F32))
    for i in range(HALO):
        for y in range(extent_y):
            at = (i * extent_y + y) * channels
            a = x_even[at : at + channels, :].astype(F32)
            b = x_odd[at : at + channels, :].astype(F32)
            put_shifted(field, i, HALO + y, jnp.where(first_x, b, a))
            put_shifted(field, HALO + extent_x + i, HALO + y, jnp.where(first_x, a, b))
    for x in range(wide_x):
        for j in range(HALO):
            at = (x * HALO + j) * channels
            a = y_even[at : at + channels, :].astype(F32)
            b = y_odd[at : at + channels, :].astype(F32)
            put_shifted(field, x, j, jnp.where(first_y, b, a))
            put_shifted(field, x, HALO + extent_y + j, jnp.where(first_y, a, b))
    for i in range(bx):
        for j in range(by):
            wide_masks[1 + i, 1 + j] = masks[i * by + j][:BRICK]
    base = HALO * extent_y * channels
    for j in range(by):
        a = x_even[base + 16 * j : base + 16 * (j + 1), :].astype(F32)[:BRICK]
        b = x_odd[base + 16 * j : base + 16 * (j + 1), :].astype(F32)[:BRICK]
        wide_masks[0, 1 + j] = jnp.where(first_x, b, a)
        wide_masks[1 + bx, 1 + j] = jnp.where(first_x, a, b)
    base = wide_x * HALO * channels
    for i in range(bx + 2):
        a = y_even[base + 16 * i : base + 16 * (i + 1), :].astype(F32)[:BRICK]
        b = y_odd[base + 16 * i : base + 16 * (i + 1), :].astype(F32)[:BRICK]
        wide_masks[i, 0] = jnp.where(first_y, b, a)
        wide_masks[i, 1 + by] = jnp.where(first_y, a, b)

    sums = jnp.zeros((channels, depth), F32)
    squares = jnp.zeros((channels, depth), F32)
    ring = 1
    block = band.shape[1] // channels
    reach = band.shape[2]
    for x in range(0, extent_x + 2 * ring, 2):
        for start in range(0, extent_y + 2 * ring, block):
            total = jnp.zeros((block * channels, 2 * depth), F32)
            for step in range(3):
                window = field[
                    start * 3 * channels : start * 3 * channels + reach,
                    (x + step) * depth : (x + step + 2) * depth,
                ]
                total = total + jnp.dot(band[step], window, preferred_element_type=F32)
            for i in range(2):
                for j in range(block):
                    at_x, at_y = x + i - ring, start + j - ring
                    mask = wide_masks[at_x // BRICK + 1, at_y // BRICK + 1][:1]
                    part = total[j * channels : (j + 1) * channels, i * depth : (i + 1) * depth]
                    value = (part * mask).astype(BF16)
                    first_out[
                        (start + j) * channels : (start + j + 1) * channels,
                        (x + i) * depth : (x + i + 1) * depth,
                    ] = value
                    if 0 <= at_x < extent_x and 0 <= at_y < extent_y:
                        value = value.astype(F32)
                        sums = sums + value
                        squares = squares + value * value
    count_mask(stats, channels, sums, squares, wide_masks, dims)


def count_mask(stats, channels, sums, squares, wide_masks, dims):
    bx, by = dims[4:]
    counts = jnp.zeros(wide_masks.shape[2:], F32)
    for i in range(bx):
        for j in range(by):
            counts = counts + wide_masks[1 + i, 1 + j] * float(BRICK)
    send_stats(stats, channels, sums, squares, counts)


def second_kernel(dims, first_out, wide_masks, received, params, band, second_out, stats, field):
    channels, extent_x, extent_y, depth, bx, by = dims
    average, scale = affine(received, params[0], channels, depth)
    shift = params[1]
    for x in range(extent_x + 2):
        for y in range(extent_y + 2):
            part = first_out[
                y * channels : (y + 1) * channels, x * depth : (x + 1) * depth
            ].astype(F32)
            mask = wide_masks[(x - 1) // BRICK + 1, (y - 1) // BRICK + 1][:1]
            part = jnp.maximum((part - average) * scale + shift, 0.0) * mask
            put_shifted(field, x, y, part)
    sums = jnp.zeros((channels, depth), F32)
    squares = jnp.zeros((channels, depth), F32)
    block = band.shape[1] // channels
    reach = band.shape[2]
    for x in range(0, extent_x, 2):
        for start in range(0, extent_y, block):
            total = jnp.zeros((block * channels, 2 * depth), F32)
            for step in range(3):
                window = field[
                    start * 3 * channels : start * 3 * channels + reach,
                    (x + step) * depth : (x + step + 2) * depth,
                ]
                total = total + jnp.dot(band[step], window, preferred_element_type=F32)
            for i in range(2):
                for j in range(block):
                    mask = wide_masks[(x + i) // BRICK + 1, (start + j) // BRICK + 1][:1]
                    part = total[j * channels : (j + 1) * channels, i * depth : (i + 1) * depth]
                    value = (part * mask).astype(BF16)
                    second_out[
                        (start + j) * channels : (start + j + 1) * channels,
                        (x + i) * depth : (x + i + 1) * depth,
                    ] = value
                    value = value.astype(F32)
                    sums = sums + value
                    squares = squares + value * value
    count_mask(stats, channels, sums, squares, wide_masks, dims)


def last_kernel(dims, second_out, wide_masks, received, params, own, result, turned):
    channels, extent_x, extent_y, depth, bx, by = dims
    average, scale = affine(received, params[2], channels, depth)
    shift = params[3]
    for x in range(extent_x):
        for j in range(by):
            mask = wide_masks[x // BRICK + 1, j + 1][:1]
            for y in range(BRICK):
                at = j * BRICK + y
                part = second_out[
                    at * channels : (at + 1) * channels, x * depth : (x + 1) * depth
                ].astype(F32)
                part = (part - average) * scale + shift + own[x, at].astype(F32)
                turned[pl.ds(y, channels, stride=BRICK), :] = jnp.maximum(part, 0.0) * mask
            result[:, x, j * BRICK : (j + 1) * BRICK, :] = (
                turned[...].reshape(channels, BRICK, depth).astype(BF16)
            )


def band_of(weight, block):
    fan_in, fan_out = weight.shape[3:]
    tall = weight.reshape(3, 9 * fan_in, fan_out).transpose(0, 2, 1)
    step = 3 * fan_in
    parts = [
        jnp.pad(tall, ((0, 0), (0, 0), (y * step, (block - 1 - y) * step))) for y in range(block)
    ]
    return jnp.concatenate(parts, axis=1)


def per_device(
    features,
    brick_mask,
    conv_first,
    conv_second,
    gain_first,
    shift_first,
    gain_second,
    shift_second,
):
    channels, extent_x, extent_y, depth = features.shape
    bx, by, bz = brick_mask.shape
    dims = (channels, extent_x, extent_y, depth, bx, by)
    devices = lax.axis_size(AXES)
    place = jnp.stack([lax.axis_index("region") % 2, lax.axis_index("strip") % 2]).astype(jnp.int32)
    wide_x = extent_x + 2 * HALO
    shape = jax.ShapeDtypeStruct

    x_rows = HALO * extent_y * channels + 16 * by
    own, masks, even, odd = call(
        functools.partial(gather_kernel, dims),
        (
            shape((extent_x, extent_y, channels, depth), BF16),
            shape((bx * by, 16, depth), F32),
            shape((x_rows, depth), BF16),
            shape((x_rows, depth), BF16),
        ),
        (place, features, brick_mask.reshape(bx * by, bz)),
        scratch=[pltpu.VMEM((channels * BRICK, depth), F32)],
        smem=1,
    )
    x_even, x_odd = swap(even, odd, "region")
    y_rows = wide_x * HALO * channels + 16 * (bx + 2)
    even, odd = call(
        functools.partial(corner_kernel, dims),
        (shape((y_rows, depth), BF16), shape((y_rows, depth), BF16)),
        (place, own, masks, x_even, x_odd),
        smem=1,
    )
    y_even, y_odd = swap(even, odd, "strip")

    first_band = band_of(conv_first, (extent_y + 2) // 2)
    second_band = band_of(conv_second, extent_y // 2)
    params = jnp.broadcast_to(
        jnp.stack([gain_first, shift_first, gain_second, shift_second])[:, :, None],
        (4, channels, depth),
    )
    first_out, wide_masks, sent = call(
        functools.partial(first_kernel, dims),
        (
            shape(((extent_y + 2) * channels, (extent_x + 2) * depth), BF16),
            shape((bx + 2, by + 2, BRICK, depth), F32),
            shape((devices, 128), F32),
        ),
        (place, own, masks, x_even, x_odd, y_even, y_odd, first_band),
        scratch=[pltpu.VMEM(((extent_y + 4) * 3 * channels, wide_x * depth), BF16)],
        smem=1,
    )
    received = lax.all_to_all(sent, AXES, 0, 0, tiled=True)
    second_out, sent = call(
        functools.partial(second_kernel, dims),
        (
            shape((extent_y * channels, extent_x * depth), BF16),
            shape((devices, 128), F32),
        ),
        (first_out, wide_masks, received, params, second_band),
        scratch=[pltpu.VMEM(((extent_y + 2) * 3 * channels, (extent_x + 2) * depth), BF16)],
    )
    received = lax.all_to_all(sent, AXES, 0, 0, tiled=True)
    return call(
        functools.partial(last_kernel, dims),
        shape(features.shape, BF16),
        (second_out, wide_masks, received, params, own),
        scratch=[pltpu.VMEM((channels * BRICK, depth), F32)],
    )


def solution(mesh):
    in_specs = (
        P(None, "region", "strip", None),
        P("region", "strip", None),
        P(),
        P(),
        P(),
        P(),
        P(),
        P(),
    )
    out_specs = P(None, "region", "strip", None)
    return jax.shard_map(
        per_device, mesh=mesh, in_specs=in_specs, out_specs=out_specs, check_vma=False
    )
```

```python
import functools

import jax
import jax.numpy as jnp
from jax import lax
from jax.experimental import pallas as pl
from jax.experimental.pallas import tpu as pltpu
from jax.sharding import PartitionSpec as P

BRICK = 8
EPSILON = 1e-05
HALO = 2
AXES = ("region", "strip")
F32 = jnp.float32
BF16 = jnp.bfloat16


def even_pairs(count):
    return [(i, i ^ 1) for i in range(count) if (i ^ 1) < count]


def odd_pairs(count):
    pairs = [(i, i + 1) for i in range(1, count - 1, 2)]
    return pairs + [(b, a) for a, b in pairs]


def swap(even, odd, axis):
    count = lax.axis_size(axis)
    return lax.ppermute(even, axis, even_pairs(count)), lax.ppermute(odd, axis, odd_pairs(count))


def whole(*_):
    return pl.BlockSpec(memory_space=pltpu.VMEM)


def call(body, outs, ins, scratch=(), flops=0, smem=0):
    in_specs = [pl.BlockSpec(memory_space=pltpu.SMEM)] * smem + [whole()] * (len(ins) - smem)
    return pl.pallas_call(
        body,
        out_shape=outs,
        in_specs=in_specs,
        out_specs=jax.tree.map(whole, outs),
        scratch_shapes=list(scratch),
        compiler_params=pltpu.CompilerParams(vmem_limit_bytes=16 << 20),
        cost_estimate=pl.CostEstimate(
            flops=flops,
            transcendentals=0,
            bytes_accessed=sum(a.size * a.dtype.itemsize for a in ins),
        ),
    )(*ins)


def brick_rows(bricks, depth):
    count = bricks.shape[1]
    at = lax.broadcasted_iota(jnp.int32, (count, depth), 0)
    voxel = lax.broadcasted_iota(jnp.int32, (count, depth), 1)
    spread = (voxel // BRICK == at).astype(F32)
    return jnp.dot(bricks, spread, preferred_element_type=F32, precision=lax.Precision.HIGHEST)


def gather_kernel(dims, place, features, bricks, own, masks, even, odd, turned):
    channels, extent_x, extent_y, depth, bx, by = dims
    rows = brick_rows(bricks[...].astype(F32), depth)
    for i in range(bx * by):
        masks[i] = jnp.broadcast_to(rows[i : i + 1], (16, depth))
    for x in range(extent_x):
        for j in range(by):
            part = features[:, x, j * BRICK : (j + 1) * BRICK, :].astype(F32)
            part = part * masks[x // BRICK * by + j][None, :BRICK, :]
            turned[...] = part.reshape(channels * BRICK, depth)
            for y in range(BRICK):
                own[x, j * BRICK + y] = turned[pl.ds(y, channels, stride=BRICK), :].astype(BF16)
    first = place[0] == 0
    for out, low in ((even, jnp.where(first, 0, 1)), (odd, jnp.where(first, 1, 0))):
        start = jnp.where(low == 1, 0, extent_x - HALO)
        for i in range(HALO):
            for y in range(extent_y):
                at = (i * extent_y + y) * channels
                out[at : at + channels, :] = own[start + i, y]
        base = HALO * extent_y * channels
        for j in range(by):
            tile = masks[jnp.where(low == 1, 0, bx - 1) * by + j]
            out[base + 16 * j : base + 16 * (j + 1), :] = tile.astype(BF16)


def corner_kernel(dims, place, own, masks, from_even, from_odd, even, odd):
    channels, extent_x, extent_y, depth, bx, by = dims
    first_x = place[0] == 0
    first_y = place[1] == 0
    wide = extent_x + 2 * HALO
    base = HALO * extent_y * channels
    for out, low in ((even, jnp.where(first_y, 0, 1)), (odd, jnp.where(first_y, 1, 0))):
        start = jnp.where(low == 1, 0, extent_y - HALO)
        brick = jnp.where(low == 1, 0, by - 1)

        def put(x, j, value):
            at = (x * HALO + j) * channels
            out[at : at + channels, :] = value

        def put_mask(x, value):
            at = wide * HALO * channels + 16 * x
            out[at : at + 16, :] = value

        for x in range(extent_x):
            for j in range(HALO):
                put(HALO + x, j, own[x, start + j])
        for x in range(bx):
            put_mask(1 + x, masks[x * by + brick].astype(BF16))
        for i in range(HALO):
            for j in range(HALO):
                at = pl.multiple_of((i * extent_y + start + j) * channels, channels)
                a = from_even[pl.ds(at, channels), :]
                b = from_odd[pl.ds(at, channels), :]
                put(i, j, jnp.where(first_x, b, a))
                put(HALO + extent_x + i, j, jnp.where(first_x, a, b))
        at = pl.multiple_of(base + brick * 16, 16)
        a = from_even[pl.ds(at, 16), :]
        b = from_odd[pl.ds(at, 16), :]
        put_mask(0, jnp.where(first_x, b, a))
        put_mask(1 + bx, jnp.where(first_x, a, b))


def put_shifted(field, x, y, value):
    channels, depth = value.shape
    lane = lax.broadcasted_iota(jnp.int32, value.shape, 1)
    before = jnp.where(lane == 0, 0.0, pltpu.roll(value, 1, 1))
    after = jnp.where(lane == depth - 1, 0.0, pltpu.roll(value, depth - 1, 1))
    for k, part in enumerate((before, value, after)):
        at = (3 * y + k) * channels
        field[at : at + channels, x * depth : (x + 1) * depth] = part.astype(BF16)


def send_stats(out, channels, sums, squares, counts):
    depth = sums.shape[1]
    rest = jnp.zeros((128 - 2 * channels - counts.shape[0], depth), F32)
    table = jnp.concatenate([sums, squares, counts, rest], axis=0)
    row = jnp.sum(jnp.transpose(table), axis=0, keepdims=True)
    out[...] = jnp.broadcast_to(row, out.shape)


def affine(stats, gain, channels, depth):
    row = jnp.sum(stats[...], axis=0, keepdims=True)
    table = jnp.transpose(jnp.broadcast_to(row, (128, 128)))
    total = jnp.sum(table[2 * channels : 2 * channels + BRICK], axis=0, keepdims=True)
    average = table[:channels] / total
    variance = table[channels : 2 * channels] / total - average * average
    return average, lax.rsqrt(variance + EPSILON) * gain


def first_kernel(
    dims, place, own, masks, x_even, x_odd, y_even, y_odd, band, first_out, wide_masks, stats, field
):
    channels, extent_x, extent_y, depth, bx, by = dims
    first_x = place[0] == 0
    first_y = place[1] == 0
    wide_x = extent_x + 2 * HALO
    for x in range(extent_x):
        for y in range(extent_y):
            put_shifted(field, HALO + x, HALO + y, own[x, y].astype(F32))
    for i in range(HALO):
        for y in range(extent_y):
            at = (i * extent_y + y) * channels
            a = x_even[at : at + channels, :].astype(F32)
            b = x_odd[at : at + channels, :].astype(F32)
            put_shifted(field, i, HALO + y, jnp.where(first_x, b, a))
            put_shifted(field, HALO + extent_x + i, HALO + y, jnp.where(first_x, a, b))
    for x in range(wide_x):
        for j in range(HALO):
            at = (x * HALO + j) * channels
            a = y_even[at : at + channels, :].astype(F32)
            b = y_odd[at : at + channels, :].astype(F32)
            put_shifted(field, x, j, jnp.where(first_y, b, a))
            put_shifted(field, x, HALO + extent_y + j, jnp.where(first_y, a, b))
    for i in range(bx):
        for j in range(by):
            wide_masks[1 + i, 1 + j] = masks[i * by + j][:BRICK]
    base = HALO * extent_y * channels
    for j in range(by):
        a = x_even[base + 16 * j : base + 16 * (j + 1), :].astype(F32)[:BRICK]
        b = x_odd[base + 16 * j : base + 16 * (j + 1), :].astype(F32)[:BRICK]
        wide_masks[0, 1 + j] = jnp.where(first_x, b, a)
        wide_masks[1 + bx, 1 + j] = jnp.where(first_x, a, b)
    base = wide_x * HALO * channels
    for i in range(bx + 2):
        a = y_even[base + 16 * i : base + 16 * (i + 1), :].astype(F32)[:BRICK]
        b = y_odd[base + 16 * i : base + 16 * (i + 1), :].astype(F32)[:BRICK]
        wide_masks[i, 0] = jnp.where(first_y, b, a)
        wide_masks[i, 1 + by] = jnp.where(first_y, a, b)

    sums = jnp.zeros((channels, depth), F32)
    squares = jnp.zeros((channels, depth), F32)
    ring = 1
    block = band.shape[1] // channels
    reach = band.shape[2]
    for x in range(0, extent_x + 2 * ring, 2):
        for start in range(0, extent_y + 2 * ring, block):
            total = jnp.zeros((block * channels, 2 * depth), F32)
            for step in range(3):
                window = field[
                    start * 3 * channels : start * 3 * channels + reach,
                    (x + step) * depth : (x + step + 2) * depth,
                ]
                total = total + jnp.dot(band[step], window, preferred_element_type=F32)
            for i in range(2):
                for j in range(block):
                    at_x, at_y = x + i - ring, start + j - ring
                    mask = wide_masks[at_x // BRICK + 1, at_y // BRICK + 1][:1]
                    part = total[j * channels : (j + 1) * channels, i * depth : (i + 1) * depth]
                    value = (part * mask).astype(BF16)
                    first_out[
                        (start + j) * channels : (start + j + 1) * channels,
                        (x + i) * depth : (x + i + 1) * depth,
                    ] = value
                    if 0 <= at_x < extent_x and 0 <= at_y < extent_y:
                        value = value.astype(F32)
                        sums = sums + value
                        squares = squares + value * value
    count_mask(stats, channels, sums, squares, wide_masks, dims)


def count_mask(stats, channels, sums, squares, wide_masks, dims):
    bx, by = dims[4:]
    counts = jnp.zeros(wide_masks.shape[2:], F32)
    for i in range(bx):
        for j in range(by):
            counts = counts + wide_masks[1 + i, 1 + j] * float(BRICK)
    send_stats(stats, channels, sums, squares, counts)


def second_kernel(dims, first_out, wide_masks, received, params, band, second_out, stats, field):
    channels, extent_x, extent_y, depth, bx, by = dims
    average, scale = affine(received, params[0], channels, depth)
    shift = params[1]
    for x in range(extent_x + 2):
        for y in range(extent_y + 2):
            part = first_out[
                y * channels : (y + 1) * channels, x * depth : (x + 1) * depth
            ].astype(F32)
            mask = wide_masks[(x - 1) // BRICK + 1, (y - 1) // BRICK + 1][:1]
            part = jnp.maximum((part - average) * scale + shift, 0.0) * mask
            put_shifted(field, x, y, part)
    sums = jnp.zeros((channels, depth), F32)
    squares = jnp.zeros((channels, depth), F32)
    block = band.shape[1] // channels
    reach = band.shape[2]
    for x in range(0, extent_x, 2):
        for start in range(0, extent_y, block):
            total = jnp.zeros((block * channels, 2 * depth), F32)
            for step in range(3):
                window = field[
                    start * 3 * channels : start * 3 * channels + reach,
                    (x + step) * depth : (x + step + 2) * depth,
                ]
                total = total + jnp.dot(band[step], window, preferred_element_type=F32)
            for i in range(2):
                for j in range(block):
                    mask = wide_masks[(x + i) // BRICK + 1, (start + j) // BRICK + 1][:1]
                    part = total[j * channels : (j + 1) * channels, i * depth : (i + 1) * depth]
                    value = (part * mask).astype(BF16)
                    second_out[
                        (start + j) * channels : (start + j + 1) * channels,
                        (x + i) * depth : (x + i + 1) * depth,
                    ] = value
                    value = value.astype(F32)
                    sums = sums + value
                    squares = squares + value * value
    count_mask(stats, channels, sums, squares, wide_masks, dims)


def last_kernel(dims, second_out, wide_masks, received, params, own, result, turned):
    channels, extent_x, extent_y, depth, bx, by = dims
    average, scale = affine(received, params[2], channels, depth)
    shift = params[3]
    for x in range(extent_x):
        for j in range(by):
            mask = wide_masks[x // BRICK + 1, j + 1][:1]
            for y in range(BRICK):
                at = j * BRICK + y
                part = second_out[
                    at * channels : (at + 1) * channels, x * depth : (x + 1) * depth
                ].astype(F32)
                part = (part - average) * scale + shift + own[x, at].astype(F32)
                turned[pl.ds(y, channels, stride=BRICK), :] = jnp.maximum(part, 0.0) * mask
            result[:, x, j * BRICK : (j + 1) * BRICK, :] = (
                turned[...].reshape(channels, BRICK, depth).astype(BF16)
            )


def band_of(weight, block):
    fan_in, fan_out = weight.shape[3:]
    tall = weight.reshape(3, 9 * fan_in, fan_out).transpose(0, 2, 1)
    step = 3 * fan_in
    parts = [
        jnp.pad(tall, ((0, 0), (0, 0), (y * step, (block - 1 - y) * step))) for y in range(block)
    ]
    return jnp.concatenate(parts, axis=1)


def per_device(
    features,
    brick_mask,
    conv_first,
    conv_second,
    gain_first,
    shift_first,
    gain_second,
    shift_second,
):
    channels, extent_x, extent_y, depth = features.shape
    bx, by, bz = brick_mask.shape
    dims = (channels, extent_x, extent_y, depth, bx, by)
    devices = lax.axis_size(AXES)
    place = jnp.stack([lax.axis_index("region") % 2, lax.axis_index("strip") % 2]).astype(jnp.int32)
    wide_x = extent_x + 2 * HALO
    shape = jax.ShapeDtypeStruct

    x_rows = HALO * extent_y * channels + 16 * by
    own, masks, even, odd = call(
        functools.partial(gather_kernel, dims),
        (
            shape((extent_x, extent_y, channels, depth), BF16),
            shape((bx * by, 16, depth), F32),
            shape((x_rows, depth), BF16),
            shape((x_rows, depth), BF16),
        ),
        (place, features, brick_mask.reshape(bx * by, bz)),
        scratch=[pltpu.VMEM((channels * BRICK, depth), F32)],
        smem=1,
    )
    x_even, x_odd = swap(even, odd, "region")
    y_rows = wide_x * HALO * channels + 16 * (bx + 2)
    even, odd = call(
        functools.partial(corner_kernel, dims),
        (shape((y_rows, depth), BF16), shape((y_rows, depth), BF16)),
        (place, own, masks, x_even, x_odd),
        smem=1,
    )
    y_even, y_odd = swap(even, odd, "strip")

    first_band = band_of(conv_first, (extent_y + 2) // 2)
    second_band = band_of(conv_second, extent_y // 2)
    params = jnp.broadcast_to(
        jnp.stack([gain_first, shift_first, gain_second, shift_second])[:, :, None],
        (4, channels, depth),
    )
    first_out, wide_masks, sent = call(
        functools.partial(first_kernel, dims),
        (
            shape(((extent_y + 2) * channels, (extent_x + 2) * depth), BF16),
            shape((bx + 2, by + 2, BRICK, depth), F32),
            shape((devices, 128), F32),
        ),
        (place, own, masks, x_even, x_odd, y_even, y_odd, first_band),
        scratch=[pltpu.VMEM(((extent_y + 4) * 3 * channels, wide_x * depth), BF16)],
        smem=1,
    )
    received = lax.all_to_all(sent, AXES, 0, 0, tiled=True)
    second_out, sent = call(
        functools.partial(second_kernel, dims),
        (
            shape((extent_y * channels, extent_x * depth), BF16),
            shape((devices, 128), F32),
        ),
        (first_out, wide_masks, received, params, second_band),
        scratch=[pltpu.VMEM(((extent_y + 2) * 3 * channels, (extent_x + 2) * depth), BF16)],
    )
    received = lax.all_to_all(sent, AXES, 0, 0, tiled=True)
    return call(
        functools.partial(last_kernel, dims),
        shape(features.shape, BF16),
        (second_out, wide_masks, received, params, own),
        scratch=[pltpu.VMEM((channels * BRICK, depth), F32)],
    )


def solution(mesh):
    in_specs = (
        P(None, "region", "strip", None),
        P("region", "strip", None),
        P(),
        P(),
        P(),
        P(),
        P(),
        P(),
    )
    out_specs = P(None, "region", "strip", None)
    return jax.shard_map(
        per_device, mesh=mesh, in_specs=in_specs, out_specs=out_specs, check_vma=False
    )
```

```python
import functools

import jax
import jax.numpy as jnp
from jax import lax
from jax.experimental import pallas as pl
from jax.experimental.pallas import tpu as pltpu
from jax.sharding import PartitionSpec as P

BRICK = 8
EPSILON = 1e-05
HALO = 2
AXES = ("region", "strip")
F32 = jnp.float32
BF16 = jnp.bfloat16


def even_pairs(count):
    return [(i, i ^ 1) for i in range(count) if (i ^ 1) < count]


def odd_pairs(count):
    pairs = [(i, i + 1) for i in range(1, count - 1, 2)]
    return pairs + [(b, a) for a, b in pairs]


def swap(even, odd, axis):
    count = lax.axis_size(axis)
    return lax.ppermute(even, axis, even_pairs(count)), lax.ppermute(odd, axis, odd_pairs(count))


def whole(*_):
    return pl.BlockSpec(memory_space=pltpu.VMEM)


def call(body, outs, ins, scratch=(), flops=0, smem=0, aliases=None):
    in_specs = [pl.BlockSpec(memory_space=pltpu.SMEM)] * smem + [whole()] * (len(ins) - smem)
    return pl.pallas_call(
        body,
        out_shape=outs,
        in_specs=in_specs,
        out_specs=jax.tree.map(whole, outs),
        scratch_shapes=list(scratch),
        input_output_aliases=aliases or {},
        compiler_params=pltpu.CompilerParams(vmem_limit_bytes=16 << 20),
        cost_estimate=pl.CostEstimate(
            flops=flops,
            transcendentals=0,
            bytes_accessed=sum(a.size * a.dtype.itemsize for a in ins),
        ),
    )(*ins)


def brick_rows(bricks, depth):
    count = bricks.shape[1]
    at = lax.broadcasted_iota(jnp.int32, (count, depth), 0)
    voxel = lax.broadcasted_iota(jnp.int32, (count, depth), 1)
    spread = (voxel // BRICK == at).astype(F32)
    return jnp.dot(bricks, spread, preferred_element_type=F32, precision=lax.Precision.HIGHEST)


def sides(place, even, odd):
    first = place == 0
    return ((even, jnp.where(first, 0, 1)), (odd, jnp.where(first, 1, 0)))


def gather_kernel(
    dims, place, features, bricks, own, masks, x_even, x_odd, y_even, y_odd, turned
):
    channels, extent_x, extent_y, depth, bx, by = dims
    rows = brick_rows(bricks[...].astype(F32), depth)
    for i in range(bx * by):
        masks[i] = jnp.broadcast_to(rows[i : i + 1], (16, depth))
    for x in range(extent_x):
        for j in range(by):
            part = features[:, x, j * BRICK : (j + 1) * BRICK, :].astype(F32)
            part = part * masks[x // BRICK * by + j][None, :BRICK, :]
            turned[...] = part.reshape(channels * BRICK, depth)
            for y in range(BRICK):
                own[x, j * BRICK + y] = turned[pl.ds(y, channels, stride=BRICK), :].astype(BF16)
    for out, low in sides(place[0], x_even, x_odd):
        start = jnp.where(low == 1, 0, extent_x - HALO)
        for i in range(HALO):
            for y in range(extent_y):
                at = (i * extent_y + y) * channels
                out[at : at + channels, :] = own[start + i, y]
        base = HALO * extent_y * channels
        for j in range(by):
            tile = masks[jnp.where(low == 1, 0, bx - 1) * by + j]
            out[base + 16 * j : base + 16 * (j + 1), :] = tile.astype(BF16)
    for out, low in sides(place[1], y_even, y_odd):
        start = jnp.where(low == 1, 0, extent_y - HALO)
        for x in range(extent_x):
            for j in range(HALO):
                at = (x * HALO + j) * channels
                out[at : at + channels, :] = own[x, start + j]
        base = extent_x * HALO * channels
        for i in range(bx):
            tile = masks[i * by + jnp.where(low == 1, 0, by - 1)]
            out[base + 16 * i : base + 16 * (i + 1), :] = tile.astype(BF16)


def corner_kernel(dims, place, x_even, x_odd, even, odd):
    channels, extent_x, extent_y, depth, bx, by = dims
    first_x = place[0] == 0
    base = HALO * extent_y * channels
    for out, low in sides(place[1], even, odd):
        start = jnp.where(low == 1, 0, extent_y - HALO)
        brick = jnp.where(low == 1, 0, by - 1)
        half = HALO * HALO * channels
        for i in range(HALO):
            for j in range(HALO):
                at = pl.multiple_of((i * extent_y + start + j) * channels, channels)
                a = x_even[pl.ds(at, channels), :]
                b = x_odd[pl.ds(at, channels), :]
                to = (i * HALO + j) * channels
                out[to : to + channels, :] = jnp.where(first_x, b, a)
                out[half + to : half + to + channels, :] = jnp.where(first_x, a, b)
        at = pl.multiple_of(base + brick * 16, 16)
        a = x_even[pl.ds(at, 16), :]
        b = x_odd[pl.ds(at, 16), :]
        out[2 * half : 2 * half + 16, :] = jnp.where(first_x, b, a)
        out[2 * half + 16 : 2 * half + 32, :] = jnp.where(first_x, a, b)


def put_shifted(field, x, y, value):
    channels, depth = value.shape
    lane = lax.broadcasted_iota(jnp.int32, value.shape, 1)
    before = jnp.where(lane == 0, 0.0, pltpu.roll(value, 1, 1))
    after = jnp.where(lane == depth - 1, 0.0, pltpu.roll(value, depth - 1, 1))
    for k, part in enumerate((before, value, after)):
        at = (3 * y + k) * channels
        field[at : at + channels, x * depth : (x + 1) * depth] = part.astype(BF16)


def send_stats(out, channels, sums, squares, counts):
    depth = sums.shape[1]
    rest = jnp.zeros((128 - 2 * channels - counts.shape[0], depth), F32)
    table = jnp.concatenate([sums, squares, counts, rest], axis=0)
    row = jnp.sum(jnp.transpose(table), axis=0, keepdims=True)
    out[...] = jnp.broadcast_to(row, out.shape)


def affine(stats, gain, channels, depth):
    row = jnp.sum(stats[...], axis=0, keepdims=True)
    table = jnp.transpose(jnp.broadcast_to(row, (128, 128)))
    total = jnp.sum(table[2 * channels : 2 * channels + BRICK], axis=0, keepdims=True)
    average = table[:channels] / total
    variance = table[channels : 2 * channels] / total - average * average
    return average, lax.rsqrt(variance + EPSILON) * gain


def fill_kernel(dims, own, field):
    extent_x, extent_y = dims[1:3]
    for x in range(extent_x):
        for y in range(extent_y):
            put_shifted(field, HALO + x, HALO + y, own[x, y].astype(F32))


def fill_halo(dims, place, edges, field):
    channels, extent_x, extent_y = dims[:3]
    first_x = place[0] == 0
    first_y = place[1] == 0
    x_even, x_odd, y_even, y_odd, c_even, c_odd = edges

    def put_pair(first, even, odd, at, low_to, high_to):
        a = even[at : at + channels, :].astype(F32)
        b = odd[at : at + channels, :].astype(F32)
        put_shifted(field, *low_to, jnp.where(first, b, a))
        put_shifted(field, *high_to, jnp.where(first, a, b))

    far_x, far_y = HALO + extent_x, HALO + extent_y
    for i in range(HALO):
        for y in range(extent_y):
            at = (i * extent_y + y) * channels
            put_pair(first_x, x_even, x_odd, at, (i, HALO + y), (far_x + i, HALO + y))
    for x in range(extent_x):
        for j in range(HALO):
            at = (x * HALO + j) * channels
            put_pair(first_y, y_even, y_odd, at, (HALO + x, j), (HALO + x, far_y + j))
    for side in range(2):
        for i in range(HALO):
            for j in range(HALO):
                at = ((side * HALO + i) * HALO + j) * channels
                x = side * far_x + i
                put_pair(first_y, c_even, c_odd, at, (x, j), (x, far_y + j))


def fill_masks(dims, place, masks, edges, wide_masks):
    channels, extent_x, extent_y, depth, bx, by = dims
    first_x = place[0] == 0
    first_y = place[1] == 0
    x_even, x_odd, y_even, y_odd, c_even, c_odd = edges

    def mask_pair(first, even, odd, at, low_to, high_to):
        a = even[at : at + 16, :].astype(F32)[:BRICK]
        b = odd[at : at + 16, :].astype(F32)[:BRICK]
        wide_masks[low_to] = jnp.where(first, b, a)
        wide_masks[high_to] = jnp.where(first, a, b)

    for i in range(bx):
        for j in range(by):
            wide_masks[1 + i, 1 + j] = masks[i * by + j][:BRICK]
    base = HALO * extent_y * channels
    for j in range(by):
        mask_pair(first_x, x_even, x_odd, base + 16 * j, (0, 1 + j), (1 + bx, 1 + j))
    base = extent_x * HALO * channels
    for i in range(bx):
        mask_pair(first_y, y_even, y_odd, base + 16 * i, (1 + i, 0), (1 + i, 1 + by))
    base = 2 * HALO * HALO * channels
    for side in range(2):
        x = side * (1 + bx)
        mask_pair(first_y, c_even, c_odd, base + 16 * side, (x, 0), (x, 1 + by))


def band_dot(band, field, x, y, rows, reach, depth):
    total = jnp.zeros((rows, 2 * depth), F32)
    channels = reach[1]
    for step in range(3):
        parts = [
            field[
                y * 3 * channels : y * 3 * channels + reach[0],
                (i + step) * depth : (i + step + 1) * depth,
            ]
            for i in x
        ]
        window = jnp.concatenate(parts, axis=1)
        total = total + jnp.dot(band[step, :rows, : reach[0]], window, preferred_element_type=F32)
    return total


def first_kernel(dims, place, filled, masks, *refs):
    edges, band, field, first_out, wide_masks, stats = refs[:6], *refs[6:]
    fill_halo(dims, place, edges, field)
    fill_masks(dims, place, masks, edges, wide_masks)
    own_outputs(dims, band, field, 1, wide_masks, first_out, stats)


def own_outputs(dims, band, field, shift, wide_masks, out, stats):
    channels, extent_x, extent_y, depth, bx, by = dims
    sums = jnp.zeros((channels, depth), F32)
    squares = jnp.zeros((channels, depth), F32)
    block = band.shape[1] // channels
    reach = (band.shape[2], channels)
    for x in range(0, extent_x, 2):
        for start in range(0, extent_y, block):
            total = band_dot(
                band,
                field,
                (x + shift, x + shift + 1),
                start + shift,
                block * channels,
                reach,
                depth,
            )
            for i in range(2):
                for j in range(block):
                    mask = wide_masks[(x + i) // BRICK + 1, (start + j) // BRICK + 1][:1]
                    part = total[j * channels : (j + 1) * channels, i * depth : (i + 1) * depth]
                    value = (part * mask).astype(BF16)
                    out[
                        (start + j) * channels : (start + j + 1) * channels,
                        (x + i) * depth : (x + i + 1) * depth,
                    ] = value
                    value = value.astype(F32)
                    sums = sums + value
                    squares = squares + value * value
    count_mask(stats, channels, sums, squares, wide_masks, dims)


def ring_kernel(dims, place, own, *refs):
    channels, extent_x, extent_y, depth, bx, by = dims
    edges, band, wide_masks, ring_y, ring_x, field = refs[:6], *refs[6:]
    fill_halo(dims, place, edges, field)
    for x in range(extent_x):
        for y in range(extent_y):
            if x == 0 or y == 0 or x == extent_x - 1 or y == extent_y - 1:
                put_shifted(field, HALO + x, HALO + y, own[x, y].astype(F32))
    for side in range(2):
        y = side * (extent_y + 1)
        for x in range(0, extent_x + 2, 2):
            total = band_dot(band, field, (x, x + 1), y, channels, (9 * channels, channels), depth)
            for i in range(2):
                mask = wide_masks[(x + i - 1) // BRICK + 1, side * (by + 1)][:1]
                part = total[:, i * depth : (i + 1) * depth] * mask
                ring_y[
                    side * channels : (side + 1) * channels, (x + i) * depth : (x + i + 1) * depth
                ] = part.astype(BF16)
    block = band.shape[1] // channels
    for start in range(0, extent_y, block):
        total = band_dot(
            band,
            field,
            (0, extent_x + 1),
            start + 1,
            block * channels,
            (band.shape[2], channels),
            depth,
        )
        for i in range(2):
            for j in range(block):
                mask = wide_masks[i * (bx + 1), (start + j) // BRICK + 1][:1]
                part = total[j * channels : (j + 1) * channels, i * depth : (i + 1) * depth]
                ring_x[
                    (start + j) * channels : (start + j + 1) * channels,
                    i * depth : (i + 1) * depth,
                ] = (part * mask).astype(BF16)


def count_mask(stats, channels, sums, squares, wide_masks, dims):
    bx, by = dims[4:]
    counts = jnp.zeros(wide_masks.shape[2:], F32)
    for i in range(bx):
        for j in range(by):
            counts = counts + wide_masks[1 + i, 1 + j] * float(BRICK)
    send_stats(stats, channels, sums, squares, counts)


def second_kernel(
    dims, first_out, ring_y, ring_x, wide_masks, received, params, band, second_out, stats, field
):
    channels, extent_x, extent_y, depth, bx, by = dims
    average, scale = affine(received, params[0], channels, depth)
    shift = params[1]

    def tile(ref, row, column):
        return ref[row * channels : (row + 1) * channels, column * depth : (column + 1) * depth]

    for x in range(extent_x + 2):
        for y in range(extent_y + 2):
            if y in (0, extent_y + 1):
                part = tile(ring_y, int(y > 0), x)
            elif x in (0, extent_x + 1):
                part = tile(ring_x, y - 1, int(x > 0))
            else:
                part = tile(first_out, y - 1, x - 1)
            mask = wide_masks[(x - 1) // BRICK + 1, (y - 1) // BRICK + 1][:1]
            part = jnp.maximum((part.astype(F32) - average) * scale + shift, 0.0) * mask
            put_shifted(field, x, y, part)
    own_outputs(dims, band, field, 0, wide_masks, second_out, stats)


def last_kernel(dims, second_out, wide_masks, received, params, own, result, turned):
    channels, extent_x, extent_y, depth, bx, by = dims
    average, scale = affine(received, params[2], channels, depth)
    shift = params[3]
    for x in range(extent_x):
        for j in range(by):
            mask = wide_masks[x // BRICK + 1, j + 1][:1]
            for y in range(BRICK):
                at = j * BRICK + y
                part = second_out[
                    at * channels : (at + 1) * channels, x * depth : (x + 1) * depth
                ].astype(F32)
                part = (part - average) * scale + shift + own[x, at].astype(F32)
                turned[pl.ds(y, channels, stride=BRICK), :] = jnp.maximum(part, 0.0) * mask
            result[:, x, j * BRICK : (j + 1) * BRICK, :] = (
                turned[...].reshape(channels, BRICK, depth).astype(BF16)
            )


def prepare_kernel(block, weights_first, weights_second, rows, first_band, second_band, params):
    for weights, band in ((weights_first, first_band), (weights_second, second_band)):
        fan_in, fan_out = weights.shape[3:]
        tall = 9 * fan_in
        wide = -(-band.shape[2] // 128) * 128
        for step in range(3):
            part = weights[step].astype(F32).reshape(tall, fan_out)
            part = jnp.concatenate([part, jnp.zeros((tall, 128 - fan_out), F32)], axis=1)
            part = jnp.concatenate([part, jnp.zeros((wide - tall, 128), F32)], axis=0)
            part = jnp.transpose(part)[:fan_out]
            for y in range(block):
                moved = part if y == 0 else pltpu.roll(part, 3 * fan_in * y, 1)
                band[step, y * fan_out : (y + 1) * fan_out, :] = moved[:, : band.shape[2]].astype(BF16)
    channels = rows.shape[1]
    for i in range(4):
        row = jnp.concatenate([rows[i : i + 1, :], jnp.zeros((1, 128 - channels), F32)], axis=1)
        params[i] = jnp.transpose(jnp.broadcast_to(row, (128, 128)))[:channels]


def per_device(
    features,
    brick_mask,
    conv_first,
    conv_second,
    gain_first,
    shift_first,
    gain_second,
    shift_second,
):
    channels, extent_x, extent_y, depth = features.shape
    bx, by, bz = brick_mask.shape
    dims = (channels, extent_x, extent_y, depth, bx, by)
    devices = lax.axis_size(AXES)
    place = jnp.stack([lax.axis_index("region") % 2, lax.axis_index("strip") % 2]).astype(jnp.int32)
    wide_x = extent_x + 2 * HALO
    shape = jax.ShapeDtypeStruct

    x_rows = HALO * extent_y * channels + 16 * by
    y_rows = HALO * extent_x * channels + 16 * bx
    c_rows = 2 * HALO * HALO * channels + 32
    own, masks, x_even, x_odd, y_even, y_odd = call(
        functools.partial(gather_kernel, dims),
        (
            shape((extent_x, extent_y, channels, depth), BF16),
            shape((bx * by, 16, depth), F32),
            shape((x_rows, depth), BF16),
            shape((x_rows, depth), BF16),
            shape((y_rows, depth), BF16),
            shape((y_rows, depth), BF16),
        ),
        (place, features, brick_mask.reshape(bx * by, bz)),
        scratch=[pltpu.VMEM((channels * BRICK, depth), F32)],
        smem=1,
    )
    x_even, x_odd = swap(x_even, x_odd, "region")
    y_even, y_odd = swap(y_even, y_odd, "strip")
    c_even, c_odd = call(
        functools.partial(corner_kernel, dims),
        (shape((c_rows, depth), BF16), shape((c_rows, depth), BF16)),
        (place, x_even, x_odd),
        smem=1,
    )
    c_even, c_odd = swap(c_even, c_odd, "strip")

    block = extent_y // 2
    band_shape = shape((3, block * channels, (block + 2) * 3 * channels), BF16)
    first_band, second_band, params = call(
        functools.partial(prepare_kernel, block),
        (band_shape, band_shape, shape((4, channels, depth), F32)),
        (
            conv_first,
            conv_second,
            jnp.stack([gain_first, shift_first, gain_second, shift_second]),
        ),
    )
    field_shape = shape(((extent_y + 2 * HALO) * 3 * channels, wide_x * depth), BF16)
    filled = call(functools.partial(fill_kernel, dims), field_shape, (own,))
    edges = (x_even, x_odd, y_even, y_odd, c_even, c_odd)
    field, first_out, wide_masks, sent = call(
        functools.partial(first_kernel, dims),
        (
            field_shape,
            shape((extent_y * channels, extent_x * depth), BF16),
            shape((bx + 2, by + 2, BRICK, depth), F32),
            shape((devices, 128), F32),
        ),
        (place, filled, masks, *edges, first_band),
        smem=1,
        aliases={1: 0},
    )
    del field
    received = lax.all_to_all(sent, AXES, 0, 0, tiled=True)
    ring_y, ring_x = call(
        functools.partial(ring_kernel, dims),
        (
            shape((2 * channels, (extent_x + 2) * depth), BF16),
            shape((extent_y * channels, 2 * depth), BF16),
        ),
        (place, own, *edges, first_band, wide_masks),
        scratch=[pltpu.VMEM(field_shape.shape, BF16)],
        smem=1,
    )
    second_out, sent = call(
        functools.partial(second_kernel, dims),
        (
            shape((extent_y * channels, extent_x * depth), BF16),
            shape((devices, 128), F32),
        ),
        (first_out, ring_y, ring_x, wide_masks, received, params, second_band),
        scratch=[pltpu.VMEM(((extent_y + 2) * 3 * channels, (extent_x + 2) * depth), BF16)],
    )
    received = lax.all_to_all(sent, AXES, 0, 0, tiled=True)
    return call(
        functools.partial(last_kernel, dims),
        shape(features.shape, BF16),
        (second_out, wide_masks, received, params, own),
        scratch=[pltpu.VMEM((channels * BRICK, depth), F32)],
    )


def solution(mesh):
    in_specs = (
        P(None, "region", "strip", None),
        P("region", "strip", None),
        P(),
        P(),
        P(),
        P(),
        P(),
        P(),
    )
    out_specs = P(None, "region", "strip", None)
    return jax.shard_map(
        per_device, mesh=mesh, in_specs=in_specs, out_specs=out_specs, check_vma=False
    )
```

```python
import functools

import jax
import jax.numpy as jnp
from jax import lax
from jax.experimental import pallas as pl
from jax.experimental.pallas import tpu as pltpu
from jax.sharding import PartitionSpec as P

BRICK = 8
EPSILON = 1e-05
HALO = 2
AXES = ("region", "strip")
F32 = jnp.float32
BF16 = jnp.bfloat16


def even_pairs(count):
    return [(i, i ^ 1) for i in range(count) if (i ^ 1) < count]


def odd_pairs(count):
    pairs = [(i, i + 1) for i in range(1, count - 1, 2)]
    return pairs + [(b, a) for a, b in pairs]


def swap(even, odd, axis):
    count = lax.axis_size(axis)
    return lax.ppermute(even, axis, even_pairs(count)), lax.ppermute(odd, axis, odd_pairs(count))


def call(body, outs, ins, scratch=(), far=(), far_out=False):
    def space(is_far):
        return pl.BlockSpec(memory_space=pltpu.HBM if is_far else pltpu.VMEM)

    return pl.pallas_call(
        body,
        out_shape=outs,
        in_specs=[space(i in far) for i in range(len(ins))],
        out_specs=jax.tree.map(lambda _: space(far_out), outs),
        scratch_shapes=list(scratch),
        compiler_params=pltpu.CompilerParams(vmem_limit_bytes=16 << 20),
        cost_estimate=pl.CostEstimate(
            flops=0,
            transcendentals=0,
            bytes_accessed=sum(a.size * a.dtype.itemsize for a in ins),
        ),
    )(*ins)


def is_even(axis):
    return lax.rem(lax.axis_index(axis), 2) == 0


def brick_rows(bricks, depth):
    count = bricks.shape[1]
    at = lax.broadcasted_iota(jnp.int32, (count, depth), 0)
    voxel = lax.broadcasted_iota(jnp.int32, (count, depth), 1)
    spread = (voxel // BRICK == at).astype(F32)
    return jnp.dot(bricks, spread, preferred_element_type=F32)


def sides(even_place, even, odd):
    return ((even, jnp.where(even_place, 0, 1)), (odd, jnp.where(even_place, 1, 0)))


def gather_kernel(dims, features, bricks, *refs):
    own, masks, x_even, x_odd, y_even, y_odd, raw, flags, turned, arrived, flags_arrived = refs
    channels, extent_x, extent_y, depth, bx, by = dims
    flag_copy = pltpu.make_async_copy(bricks, flags, flags_arrived)
    flag_copy.start()
    copies = []
    for x in range(0, extent_x, 2):
        copy = pltpu.make_async_copy(
            features.at[:, x : x + 2], raw.at[:, x : x + 2], arrived.at[x // 2]
        )
        copy.start()
        copies.append(copy)
    flag_copy.wait()
    rows = brick_rows(flags[...].astype(F32), depth)
    for i in range(bx * by):
        masks[i] = jnp.broadcast_to(rows[i : i + 1], (16, depth))
    for x in range(extent_x):
        if x % 2 == 0:
            copies[x // 2].wait()
        for j in range(by):
            part = raw[:, x, j * BRICK : (j + 1) * BRICK, :].astype(F32)
            part = part * masks[x // BRICK * by + j][None, :BRICK, :]
            turned[x % 2] = part.reshape(channels * BRICK, depth)
            for y in range(BRICK):
                own[x, j * BRICK + y] = turned[x % 2, pl.ds(y, channels, stride=BRICK), :].astype(
                    BF16
                )
    for out, low in sides(is_even("region"), x_even, x_odd):
        start = jnp.where(low == 1, 0, extent_x - HALO)
        for i in range(HALO):
            for y in range(extent_y):
                at = (i * extent_y + y) * channels
                out[at : at + channels, :] = own[start + i, y]
        base = HALO * extent_y * channels
        for j in range(by):
            tile = masks[jnp.where(low == 1, 0, bx - 1) * by + j]
            out[base + 16 * j : base + 16 * (j + 1), :] = tile.astype(BF16)
    for out, low in sides(is_even("strip"), y_even, y_odd):
        start = jnp.where(low == 1, 0, extent_y - HALO)
        for x in range(extent_x):
            for j in range(HALO):
                at = (x * HALO + j) * channels
                out[at : at + channels, :] = own[x, start + j]
        base = extent_x * HALO * channels
        for i in range(bx):
            tile = masks[i * by + jnp.where(low == 1, 0, by - 1)]
            out[base + 16 * i : base + 16 * (i + 1), :] = tile.astype(BF16)


def corner_kernel(dims, x_even, x_odd, even, odd):
    channels, extent_x, extent_y, depth, bx, by = dims
    first_x = is_even("region")
    base = HALO * extent_y * channels
    for out, low in sides(is_even("strip"), even, odd):
        start = jnp.where(low == 1, 0, extent_y - HALO)
        brick = jnp.where(low == 1, 0, by - 1)
        half = HALO * HALO * channels
        for i in range(HALO):
            for j in range(HALO):
                at = pl.multiple_of((i * extent_y + start + j) * channels, channels)
                a = x_even[pl.ds(at, channels), :]
                b = x_odd[pl.ds(at, channels), :]
                to = (i * HALO + j) * channels
                out[to : to + channels, :] = jnp.where(first_x, b, a)
                out[half + to : half + to + channels, :] = jnp.where(first_x, a, b)
        at = pl.multiple_of(base + brick * 16, 16)
        a = x_even[pl.ds(at, 16), :]
        b = x_odd[pl.ds(at, 16), :]
        out[2 * half : 2 * half + 16, :] = jnp.where(first_x, b, a)
        out[2 * half + 16 : 2 * half + 32, :] = jnp.where(first_x, a, b)


def prepare_kernel(weights_first, weights_second, rows, first_band, second_band, params):
    for weights, band in ((weights_first, first_band), (weights_second, second_band)):
        fan_in, fan_out = weights.shape[3:]
        wide = 4 * fan_in
        blank = jnp.zeros((fan_out, wide), BF16)
        for dz in range(3):
            pieces = []
            for dx in range(3):
                part = jnp.concatenate([weights[dx, dy, dz].astype(F32) for dy in range(3)], axis=0)
                part = jnp.concatenate([part, jnp.zeros((fan_in, fan_out), F32)], axis=0)
                part = jnp.concatenate([part, jnp.zeros((wide, 128 - fan_out), F32)], axis=1)
                part = jnp.transpose(part)[:fan_out]
                pieces.append((part.astype(BF16), pltpu.roll(part, fan_in, 1).astype(BF16)))
            for x in range(2):
                for y in range(2):
                    at = ((dz * 2 + x) * 2 + y) * fan_out
                    for i in range(4):
                        piece = pieces[i - x][y] if 0 <= i - x < 3 else blank
                        band[at : at + fan_out, i * wide : (i + 1) * wide] = piece
    channels = rows.shape[1]
    for i in range(4):
        row = jnp.concatenate([rows[i : i + 1, :], jnp.zeros((1, 128 - channels), F32)], axis=1)
        params[i] = jnp.transpose(jnp.broadcast_to(row, (128, 128)))[:channels]


def convolve_groups(groups, column, band, channels, depth, emit):
    lane = lax.broadcasted_iota(jnp.int32, (channels, depth), 1)
    at_start, at_end = lane == 0, lane == depth - 1
    for i in range(0, len(groups), 2):
        pair = groups[i : i + 2]
        windows = []
        for x, y in pair:
            parts = [column(x + a - 1, y + b - 1) for a in range(4) for b in range(4)]
            windows.append(jnp.concatenate(parts, axis=0))
        window = jnp.concatenate(windows, axis=1) if len(windows) > 1 else windows[0]
        total = jnp.dot(band[...], window, preferred_element_type=F32)
        for n, (x, y) in enumerate(pair):
            for a in range(2):
                for b in range(2):
                    before, here, after = (
                        total[
                            ((dz * 2 + a) * 2 + b) * channels : ((dz * 2 + a) * 2 + b + 1)
                            * channels,
                            n * depth : (n + 1) * depth,
                        ]
                        for dz in range(3)
                    )
                    before = jnp.where(at_start, 0.0, pltpu.roll(before, 1, 1))
                    after = jnp.where(at_end, 0.0, pltpu.roll(after, depth - 1, 1))
                    emit(x + a, y + b, here + before + after)


def send_stats(out, channels, sums, squares, counts):
    depth = sums.shape[1]
    rest = jnp.zeros((128 - 2 * channels - counts.shape[0], depth), F32)
    table = jnp.concatenate([sums, squares, counts, rest], axis=0)
    row = jnp.sum(jnp.transpose(table), axis=0, keepdims=True)
    out[...] = jnp.broadcast_to(row, out.shape)


def affine(stats, gain, channels, depth):
    row = jnp.sum(stats[...], axis=0, keepdims=True)
    table = jnp.transpose(jnp.broadcast_to(row, (128, 128)))
    total = jnp.sum(table[2 * channels : 2 * channels + BRICK], axis=0, keepdims=True)
    average = table[:channels] / total
    variance = table[channels : 2 * channels] / total - average * average
    return average, lax.rsqrt(variance + EPSILON) * gain


class Edges:
    def __init__(self, dims, own, masks, x_pair, y_pair, corner_pair=None):
        self.dims = dims
        self.own, self.masks = own, masks
        self.x_pair, self.y_pair, self.corner_pair = x_pair, y_pair, corner_pair
        self.first_x, self.first_y = is_even("region"), is_even("strip")

    def pick(self, pair, first, low, at, rows):
        even, odd = (ref[at : at + rows, :] for ref in pair)
        return jnp.where(first, odd, even) if low else jnp.where(first, even, odd)

    def column(self, x, y):
        channels, extent_x, extent_y = self.dims[:3]
        inside_x, inside_y = 0 <= x < extent_x, 0 <= y < extent_y
        if inside_x and inside_y:
            return self.own[x, y]
        i = x + HALO if x < 0 else x - extent_x
        j = y + HALO if y < 0 else y - extent_y
        if inside_y:
            at = (i * extent_y + y) * channels
            return self.pick(self.x_pair, self.first_x, x < 0, at, channels)
        if inside_x:
            at = (x * HALO + j) * channels
            return self.pick(self.y_pair, self.first_y, y < 0, at, channels)
        at = ((int(x > 0) * HALO + i) * HALO + j) * channels
        return self.pick(self.corner_pair, self.first_y, y < 0, at, channels)

    def mask(self, i, j):
        channels, extent_x, extent_y, depth, bx, by = self.dims
        inside_x, inside_y = 0 <= i < bx, 0 <= j < by
        if inside_x and inside_y:
            return self.masks[i * by + j][:BRICK]
        if inside_y:
            at = HALO * extent_y * channels + 16 * j
            tile = self.pick(self.x_pair, self.first_x, i < 0, at, 16)
        elif inside_x:
            at = HALO * extent_x * channels + 16 * i
            tile = self.pick(self.y_pair, self.first_y, j < 0, at, 16)
        else:
            at = 2 * HALO * HALO * channels + 16 * int(i > 0)
            tile = self.pick(self.corner_pair, self.first_y, j < 0, at, 16)
        return tile.astype(F32)[:BRICK]


class Sums:
    def __init__(self, sums, squares):
        self.sums, self.squares = sums, squares

    def add(self, value):
        value = value.astype(F32)
        self.sums = self.sums + value
        self.squares = self.squares + value * value


def ring_groups(extent_x, extent_y):
    far = (extent_x - 1, extent_y - 1)
    groups = [(x, y) for x in range(-1, extent_x, 2) for y in range(-1, extent_y, 2)]
    corners = [g for g in groups if g[0] in (-1, far[0]) and g[1] in (-1, far[1])]
    return [g for g in groups if g not in corners], corners


def first_kernel(dims, own, masks, x_even, x_odd, y_even, y_odd, band, first_out, partial):
    channels, extent_x, extent_y, depth, bx, by = dims
    edges = Edges(dims, own, masks, (x_even, x_odd), (y_even, y_odd))
    found = {}
    zero = jnp.zeros((channels, depth), F32)
    sums = Sums(zero, zero)

    def emit(x, y, value):
        brick = (x // BRICK, y // BRICK)
        if brick not in found:
            found[brick] = edges.mask(*brick)[:1]
        value = (value * found[brick]).astype(BF16)
        first_out[x + 1, y + 1] = value
        if 0 <= x < extent_x and 0 <= y < extent_y:
            sums.add(value)

    groups = ring_groups(extent_x, extent_y)[0]
    convolve_groups(groups, edges.column, band, channels, depth, emit)
    partial[0] = sums.sums
    partial[1] = sums.squares


def finish_kernel(dims, own, masks, *refs):
    x_even, x_odd, y_even, y_odd, c_even, c_odd, band, partial, corner_out, wide_masks, stats = refs
    channels, extent_x, extent_y, depth, bx, by = dims
    edges = Edges(dims, own, masks, (x_even, x_odd), (y_even, y_odd), (c_even, c_odd))
    counts = jnp.zeros((BRICK, depth), F32)
    for i in range(-1, bx + 1):
        for j in range(-1, by + 1):
            tile = edges.mask(i, j)
            wide_masks[i + 1, j + 1] = tile
            if 0 <= i < bx and 0 <= j < by:
                counts = counts + tile * float(BRICK)
    sums = Sums(partial[0], partial[1])

    def emit(x, y, value):
        value = (value * edges.mask(x // BRICK, y // BRICK)[:1]).astype(BF16)
        side_x, side_y = int(x > 0 and x >= extent_x - 1), int(y > 0 and y >= extent_y - 1)
        i = x - (extent_x - 1 if side_x else -1)
        j = y - (extent_y - 1 if side_y else -1)
        corner_out[2 * side_x + i, 2 * side_y + j] = value
        if 0 <= x < extent_x and 0 <= y < extent_y:
            sums.add(value)

    groups = ring_groups(extent_x, extent_y)[1]
    convolve_groups(groups, edges.column, band, channels, depth, emit)
    send_stats(stats, channels, sums.sums, sums.squares, counts)


def second_kernel(dims, *refs):
    first_out, corner_out, wide_masks, received, params, band, second_out, stats, field = refs
    channels, extent_x, extent_y, depth, bx, by = dims
    average, scale = affine(received, params[0], channels, depth)
    shift = params[1]
    edge_x, edge_y = (0, 1, extent_x, extent_x + 1), (0, 1, extent_y, extent_y + 1)
    for x in range(extent_x + 2):
        for y in range(extent_y + 2):
            if x in edge_x and y in edge_y:
                part = corner_out[edge_x.index(x), edge_y.index(y)]
            else:
                part = first_out[x, y]
            mask = wide_masks[(x - 1) // BRICK + 1, (y - 1) // BRICK + 1][:1]
            part = jnp.maximum((part.astype(F32) - average) * scale + shift, 0.0) * mask
            field[x, y] = part.astype(BF16)
    zero = jnp.zeros((channels, depth), F32)
    sums = Sums(zero, zero)

    def emit(x, y, value):
        value = (value * wide_masks[x // BRICK + 1, y // BRICK + 1][:1]).astype(BF16)
        second_out[x, y] = value
        sums.add(value)

    groups = [(x, y) for x in range(0, extent_x, 2) for y in range(0, extent_y, 2)]
    convolve_groups(
        groups, lambda x, y: field[x + 1, y + 1], band, channels, depth, emit
    )
    counts = jnp.zeros((BRICK, depth), F32)
    for i in range(bx):
        for j in range(by):
            counts = counts + wide_masks[1 + i, 1 + j] * float(BRICK)
    send_stats(stats, channels, sums.sums, sums.squares, counts)


def last_kernel(dims, second_out, wide_masks, received, params, own, result, turned, ready, sent):
    channels, extent_x, extent_y, depth, bx, by = dims
    average, scale = affine(received, params[2], channels, depth)
    shift = params[3]
    copies = []
    for x in range(extent_x):
        for j in range(by):
            mask = wide_masks[x // BRICK + 1, j + 1][:1]
            for y in range(BRICK):
                at = j * BRICK + y
                part = second_out[x, at].astype(F32)
                part = (part - average) * scale + shift + own[x, at].astype(F32)
                part = jnp.maximum(part, 0.0) * mask
                turned[x % 2, pl.ds(y, channels, stride=BRICK), :] = part
            ready[:, x, j * BRICK : (j + 1) * BRICK, :] = (
                turned[x % 2].reshape(channels, BRICK, depth).astype(BF16)
            )
        if x % 2 == 1:
            copy = pltpu.make_async_copy(
                ready.at[:, x - 1 : x + 1], result.at[:, x - 1 : x + 1], sent.at[x // 2]
            )
            copy.start()
            copies.append(copy)
    for copy in copies:
        copy.wait()


def per_device(
    features,
    brick_mask,
    conv_first,
    conv_second,
    gain_first,
    shift_first,
    gain_second,
    shift_second,
):
    channels, extent_x, extent_y, depth = features.shape
    bx, by, bz = brick_mask.shape
    dims = (channels, extent_x, extent_y, depth, bx, by)
    devices = lax.axis_size(AXES)
    shape = jax.ShapeDtypeStruct

    x_rows = HALO * extent_y * channels + 16 * by
    y_rows = HALO * extent_x * channels + 16 * bx
    c_rows = 2 * HALO * HALO * channels + 32
    own, masks, x_even, x_odd, y_even, y_odd = call(
        functools.partial(gather_kernel, dims),
        (
            shape((extent_x, extent_y, channels, depth), BF16),
            shape((bx * by, 16, depth), F32),
            shape((x_rows, depth), BF16),
            shape((x_rows, depth), BF16),
            shape((y_rows, depth), BF16),
            shape((y_rows, depth), BF16),
        ),
        (
            pltpu.with_memory_space_constraint(features, pltpu.HBM),
            pltpu.with_memory_space_constraint(brick_mask.reshape(bx * by, bz), pltpu.HBM),
        ),
        scratch=[
            pltpu.VMEM(features.shape, BF16),
            pltpu.VMEM((bx * by, bz), jnp.int32),
            pltpu.VMEM((2, channels * BRICK, depth), F32),
            pltpu.SemaphoreType.DMA((extent_x // 2,)),
            pltpu.SemaphoreType.DMA,
        ],
        far=(0, 1),
    )
    x_pair = swap(x_even, x_odd, "region")
    y_pair = swap(y_even, y_odd, "strip")
    corners = call(
        functools.partial(corner_kernel, dims),
        (shape((c_rows, depth), BF16), shape((c_rows, depth), BF16)),
        x_pair,
    )
    c_pair = swap(*corners, "strip")

    band_shape = shape((12 * channels, 16 * channels), BF16)
    first_band, second_band, params = call(
        prepare_kernel,
        (band_shape, band_shape, shape((4, channels, depth), F32)),
        (
            conv_first,
            conv_second,
            jnp.stack([gain_first, shift_first, gain_second, shift_second]),
        ),
    )
    wide_shape = (extent_x + 2, extent_y + 2, channels, depth)
    first_out, partial = call(
        functools.partial(first_kernel, dims),
        (shape(wide_shape, BF16), shape((2, channels, depth), F32)),
        (own, masks, *x_pair, *y_pair, first_band),
    )
    corner_out, wide_masks, sent = call(
        functools.partial(finish_kernel, dims),
        (
            shape((4, 4, channels, depth), BF16),
            shape((bx + 2, by + 2, BRICK, depth), F32),
            shape((devices, 128), F32),
        ),
        (own, masks, *x_pair, *y_pair, *c_pair, first_band, partial),
    )
    received = lax.all_to_all(sent, AXES, 0, 0, tiled=True)
    second_out, sent = call(
        functools.partial(second_kernel, dims),
        (
            shape((extent_x, extent_y, channels, depth), BF16),
            shape((devices, 128), F32),
        ),
        (first_out, corner_out, wide_masks, received, params, second_band),
        scratch=[pltpu.VMEM(wide_shape, BF16)],
    )
    received = lax.all_to_all(sent, AXES, 0, 0, tiled=True)
    return call(
        functools.partial(last_kernel, dims),
        shape(features.shape, BF16),
        (second_out, wide_masks, received, params, own),
        scratch=[
            pltpu.VMEM((2, channels * BRICK, depth), F32),
            pltpu.VMEM(features.shape, BF16),
            pltpu.SemaphoreType.DMA((extent_x // 2,)),
        ],
        far_out=True,
    )


def solution(mesh):
    in_specs = (
        P(None, "region", "strip", None),
        P("region", "strip", None),
        P(),
        P(),
        P(),
        P(),
        P(),
        P(),
    )
    out_specs = P(None, "region", "strip", None)
    return jax.shard_map(
        per_device, mesh=mesh, in_specs=in_specs, out_specs=out_specs, check_vma=False
    )
```

```python
import functools

import jax
import jax.numpy as jnp
from jax import lax
from jax.experimental import pallas as pl
from jax.experimental.pallas import tpu as pltpu
from jax.sharding import PartitionSpec as P

BRICK = 8
EPSILON = 1e-05
HALO = 2
AXES = ("region", "strip")
F32 = jnp.float32
BF16 = jnp.bfloat16


def even_pairs(count):
    return [(i, i ^ 1) for i in range(count) if (i ^ 1) < count]


def odd_pairs(count):
    pairs = [(i, i + 1) for i in range(1, count - 1, 2)]
    return pairs + [(b, a) for a, b in pairs]


def swap(even, odd, axis):
    count = lax.axis_size(axis)
    odd = lax.ppermute(odd, axis, odd_pairs(count))
    return lax.ppermute(even, axis, even_pairs(count)), odd


def call(body, outs, ins, scratch=(), far=(), far_out=False):
    def space(is_far):
        return pl.BlockSpec(memory_space=pltpu.HBM if is_far else pltpu.VMEM)

    return pl.pallas_call(
        body,
        out_shape=outs,
        in_specs=[space(i in far) for i in range(len(ins))],
        out_specs=jax.tree.map(lambda _: space(far_out), outs),
        scratch_shapes=list(scratch),
        compiler_params=pltpu.CompilerParams(vmem_limit_bytes=16 << 20),
        cost_estimate=pl.CostEstimate(
            flops=0,
            transcendentals=0,
            bytes_accessed=sum(a.size * a.dtype.itemsize for a in ins),
        ),
    )(*ins)


def is_even(axis):
    return lax.rem(lax.axis_index(axis), 2) == 0


def brick_rows(bricks, depth):
    count = bricks.shape[1]
    at = lax.broadcasted_iota(jnp.int32, (count, depth), 0)
    voxel = lax.broadcasted_iota(jnp.int32, (count, depth), 1)
    spread = (voxel // BRICK == at).astype(F32)
    return jnp.dot(bricks, spread, preferred_element_type=F32)


def sides(even_place, even, odd):
    return ((even, jnp.where(even_place, 0, 1)), (odd, jnp.where(even_place, 1, 0)))


def turn(dims, raw, x, raw_x, masks, turned, keep):
    channels, extent_x, extent_y, depth, bx, by = dims
    for j in range(by):
        part = raw[:, raw_x, j * BRICK : (j + 1) * BRICK, :].astype(F32)
        part = part * masks[x // BRICK * by + j][None]
        turned[x % 2] = part.reshape(channels * BRICK, depth)
        for y in range(BRICK):
            value = turned[x % 2, pl.ds(y, channels, stride=BRICK), :]
            keep(j * BRICK + y, value.astype(BF16))


def edge_kernel(dims, features, bricks, *refs):
    masks, even, odd, raw, flags, turned, edge, arrived, flags_arrived = refs
    channels, extent_x, extent_y, depth, bx, by = dims
    flag_copy = pltpu.make_async_copy(bricks, flags, flags_arrived)
    flag_copy.start()
    copies = []
    for side in range(2):
        start = side * (extent_x - HALO)
        copy = pltpu.make_async_copy(
            features.at[:, start : start + HALO], raw.at[side], arrived.at[side]
        )
        copy.start()
        copies.append(copy)
    flag_copy.wait()
    rows = brick_rows(flags[...].astype(F32), depth)
    for i in range(bx * by):
        masks[i] = jnp.broadcast_to(rows[i : i + 1], (BRICK, depth))
    for side in range(2):
        copies[side].wait()
        for i in range(HALO):

            def keep(y, value):
                at = (i * extent_y + y) * channels
                edge[1 - side, at : at + channels, :] = value

            turn(dims, raw.at[side], side * (extent_x - HALO) + i, i, masks, turned, keep)
    rows = HALO * extent_y * channels
    for out, low in sides(is_even("region"), even, odd):
        out[:rows, :] = edge[low]
        for j in range(by):
            tile = masks[jnp.where(low == 1, 0, bx - 1) * by + j]
            out[rows + BRICK * j : rows + BRICK * (j + 1), :] = tile.astype(BF16)


def gather_kernel(dims, features, masks, own, even, odd, turned):
    channels, extent_x, extent_y, depth, bx, by = dims
    for x in range(extent_x):

        def keep(y, value):
            own[x, y] = value

        turn(dims, features, x, x, masks, turned, keep)
    for out, low in sides(is_even("strip"), even, odd):
        start = jnp.where(low == 1, 0, extent_y - HALO)
        for x in range(extent_x):
            for j in range(HALO):
                at = (x * HALO + j) * channels
                out[at : at + channels, :] = own[x, start + j]
        base = extent_x * HALO * channels
        for i in range(bx):
            tile = masks[i * by + jnp.where(low == 1, 0, by - 1)]
            out[base + BRICK * i : base + BRICK * (i + 1), :] = tile.astype(BF16)


def corner_kernel(dims, x_even, x_odd, even, odd):
    channels, extent_x, extent_y, depth, bx, by = dims
    first_x = is_even("region")
    base = HALO * extent_y * channels
    for out, low in sides(is_even("strip"), even, odd):
        start = jnp.where(low == 1, 0, extent_y - HALO)
        brick = jnp.where(low == 1, 0, by - 1)
        half = HALO * HALO * channels
        for i in range(HALO):
            for j in range(HALO):
                at = pl.multiple_of((i * extent_y + start + j) * channels, channels)
                a = x_even[pl.ds(at, channels), :]
                b = x_odd[pl.ds(at, channels), :]
                to = (i * HALO + j) * channels
                out[to : to + channels, :] = jnp.where(first_x, b, a)
                out[half + to : half + to + channels, :] = jnp.where(first_x, a, b)
        at = pl.multiple_of(base + brick * BRICK, BRICK)
        a = x_even[pl.ds(at, BRICK), :].astype(F32)
        b = x_odd[pl.ds(at, BRICK), :].astype(F32)
        tiles = (jnp.where(first_x, b, a), jnp.where(first_x, a, b))
        out[2 * half : 2 * half + 2 * BRICK, :] = jnp.concatenate(tiles, axis=0).astype(BF16)


def prepare_kernel(weights_first, weights_second, rows, first_band, second_band, params):
    for weights, band in ((weights_first, first_band), (weights_second, second_band)):
        fan_in, fan_out = weights.shape[3:]
        wide = 4 * fan_in
        blank = jnp.zeros((fan_out, wide), BF16)
        for dz in range(3):
            pieces = []
            for dx in range(3):
                part = jnp.concatenate([weights[dx, dy, dz].astype(F32) for dy in range(3)], axis=0)
                part = jnp.concatenate([part, jnp.zeros((fan_in, fan_out), F32)], axis=0)
                part = jnp.concatenate([part, jnp.zeros((wide, 128 - fan_out), F32)], axis=1)
                part = jnp.transpose(part)[:fan_out]
                pieces.append((part.astype(BF16), pltpu.roll(part, fan_in, 1).astype(BF16)))
            for x in range(2):
                for y in range(2):
                    at = ((dz * 2 + x) * 2 + y) * fan_out
                    for i in range(4):
                        piece = pieces[i - x][y] if 0 <= i - x < 3 else blank
                        band[at : at + fan_out, i * wide : (i + 1) * wide] = piece
    channels = rows.shape[1]
    for i in range(4):
        row = jnp.concatenate([rows[i : i + 1, :], jnp.zeros((1, 128 - channels), F32)], axis=1)
        params[i] = jnp.transpose(jnp.broadcast_to(row, (128, 128)))[:channels]


def window_of(group):
    return [(group[0] + a - 1, group[1] + b - 1) for a in range(4) for b in range(4)]


def convolve_groups(groups, column, band, channels, depth, emit, ready=None):
    pairs = [groups[i : i + 2] for i in range(0, len(groups), 2)]

    def prepare(i):
        if ready is not None and i < len(pairs):
            for group in pairs[i]:
                for x, y in window_of(group):
                    ready(x, y)

    prepare(0)
    lane = lax.broadcasted_iota(jnp.int32, (channels, depth), 1)
    at_start, at_end = lane == 0, lane == depth - 1
    for i, pair in enumerate(pairs):
        windows = [jnp.concatenate([column(*at) for at in window_of(g)], axis=0) for g in pair]
        window = jnp.concatenate(windows, axis=1) if len(windows) > 1 else windows[0]
        total = jnp.dot(band[...], window, preferred_element_type=F32)
        prepare(i + 1)
        for n, (x, y) in enumerate(pair):
            for a in range(2):
                for b in range(2):
                    before, here, after = (
                        total[
                            ((dz * 2 + a) * 2 + b) * channels : ((dz * 2 + a) * 2 + b + 1)
                            * channels,
                            n * depth : (n + 1) * depth,
                        ]
                        for dz in range(3)
                    )
                    before = jnp.where(at_start, 0.0, pltpu.roll(before, 1, 1))
                    after = jnp.where(at_end, 0.0, pltpu.roll(after, depth - 1, 1))
                    emit(x + a, y + b, here + before + after)


def send_stats(out, channels, sums, squares, counts):
    depth = sums.shape[1]
    rest = jnp.zeros((128 - 2 * channels - counts.shape[0], depth), F32)
    table = jnp.concatenate([sums, squares, counts, rest], axis=0)
    row = jnp.sum(jnp.transpose(table), axis=0, keepdims=True)
    out[...] = jnp.broadcast_to(row, out.shape)


def affine(stats, gain, channels, depth):
    row = jnp.sum(stats[...], axis=0, keepdims=True)
    table = jnp.transpose(jnp.broadcast_to(row, (128, 128)))
    total = jnp.sum(table[2 * channels : 2 * channels + BRICK], axis=0, keepdims=True)
    average = table[:channels] / total
    variance = table[channels : 2 * channels] / total - average * average
    return average, lax.rsqrt(variance + EPSILON) * gain


class Edges:
    def __init__(self, dims, own, masks, x_pair, y_pair, corner_pair=None):
        self.dims = dims
        self.own, self.masks = own, masks
        self.x_pair, self.y_pair, self.corner_pair = x_pair, y_pair, corner_pair
        self.first_x, self.first_y = is_even("region"), is_even("strip")

    def pick(self, pair, first, low, at, rows):
        even, odd = (ref[at : at + rows, :] for ref in pair)
        if rows == BRICK:
            even, odd = even.astype(F32), odd.astype(F32)
        return jnp.where(first, odd, even) if low else jnp.where(first, even, odd)

    def column(self, x, y):
        channels, extent_x, extent_y = self.dims[:3]
        inside_x, inside_y = 0 <= x < extent_x, 0 <= y < extent_y
        if inside_x and inside_y:
            return self.own[x, y]
        i = x + HALO if x < 0 else x - extent_x
        j = y + HALO if y < 0 else y - extent_y
        if inside_y:
            at = (i * extent_y + y) * channels
            return self.pick(self.x_pair, self.first_x, x < 0, at, channels)
        if inside_x:
            at = (x * HALO + j) * channels
            return self.pick(self.y_pair, self.first_y, y < 0, at, channels)
        at = ((int(x > 0) * HALO + i) * HALO + j) * channels
        return self.pick(self.corner_pair, self.first_y, y < 0, at, channels)

    def mask(self, i, j):
        channels, extent_x, extent_y, depth, bx, by = self.dims
        inside_x, inside_y = 0 <= i < bx, 0 <= j < by
        if inside_x and inside_y:
            return self.masks[i * by + j]
        if inside_y:
            at = HALO * extent_y * channels + BRICK * j
            tile = self.pick(self.x_pair, self.first_x, i < 0, at, BRICK)
        elif inside_x:
            at = HALO * extent_x * channels + BRICK * i
            tile = self.pick(self.y_pair, self.first_y, j < 0, at, BRICK)
        else:
            at = 2 * HALO * HALO * channels + BRICK * int(i > 0)
            tile = self.pick(self.corner_pair, self.first_y, j < 0, at, BRICK)
        return tile


class Sums:
    def __init__(self, sums, squares):
        self.sums, self.squares = sums, squares

    def add(self, value):
        value = value.astype(F32)
        self.sums = self.sums + value
        self.squares = self.squares + value * value


def ring_groups(extent_x, extent_y):
    far = (extent_x - 1, extent_y - 1)
    groups = [(x, y) for x in range(-1, extent_x, 2) for y in range(-1, extent_y, 2)]
    corners = [g for g in groups if g[0] in (-1, far[0]) and g[1] in (-1, far[1])]
    return [g for g in groups if g not in corners], corners


def first_kernel(dims, own, masks, x_even, x_odd, y_even, y_odd, band, first_out, partial):
    channels, extent_x, extent_y, depth, bx, by = dims
    edges = Edges(dims, own, masks, (x_even, x_odd), (y_even, y_odd))
    found = {}
    zero = jnp.zeros((channels, depth), F32)
    sums = Sums(zero, zero)

    def emit(x, y, value):
        brick = (x // BRICK, y // BRICK)
        if brick not in found:
            found[brick] = edges.mask(*brick)[:1]
        value = (value * found[brick]).astype(BF16)
        first_out[x + 1, y + 1] = value
        if 0 <= x < extent_x and 0 <= y < extent_y:
            sums.add(value)

    groups = ring_groups(extent_x, extent_y)[0]
    convolve_groups(groups, edges.column, band, channels, depth, emit)
    partial[0] = sums.sums
    partial[1] = sums.squares


def finish_kernel(dims, own, masks, *refs):
    x_even, x_odd, y_even, y_odd, c_even, c_odd, band, partial, corner_out, wide_masks, stats = refs
    channels, extent_x, extent_y, depth, bx, by = dims
    edges = Edges(dims, own, masks, (x_even, x_odd), (y_even, y_odd), (c_even, c_odd))
    counts = jnp.zeros((BRICK, depth), F32)
    for i in range(-1, bx + 1):
        for j in range(-1, by + 1):
            tile = edges.mask(i, j)
            wide_masks[i + 1, j + 1] = tile
            if 0 <= i < bx and 0 <= j < by:
                counts = counts + tile * float(BRICK)
    sums = Sums(partial[0], partial[1])

    def emit(x, y, value):
        value = (value * edges.mask(x // BRICK, y // BRICK)[:1]).astype(BF16)
        side_x, side_y = int(x > 0 and x >= extent_x - 1), int(y > 0 and y >= extent_y - 1)
        i = x - (extent_x - 1 if side_x else -1)
        j = y - (extent_y - 1 if side_y else -1)
        corner_out[2 * side_x + i, 2 * side_y + j] = value
        if 0 <= x < extent_x and 0 <= y < extent_y:
            sums.add(value)

    groups = ring_groups(extent_x, extent_y)[1]
    convolve_groups(groups, edges.column, band, channels, depth, emit)
    send_stats(stats, channels, sums.sums, sums.squares, counts)


def second_kernel(dims, *refs):
    first_out, corner_out, wide_masks, received, params, band, second_out, stats, field = refs
    channels, extent_x, extent_y, depth, bx, by = dims
    average, scale = affine(received, params[0], channels, depth)
    shift = params[1]
    edge_x, edge_y = (0, 1, extent_x, extent_x + 1), (0, 1, extent_y, extent_y + 1)
    done = set()

    def activate(x, y):
        if (x, y) in done:
            return
        done.add((x, y))
        if x + 1 in edge_x and y + 1 in edge_y:
            part = corner_out[edge_x.index(x + 1), edge_y.index(y + 1)]
        else:
            part = first_out[x + 1, y + 1]
        mask = wide_masks[x // BRICK + 1, y // BRICK + 1][:1]
        part = jnp.maximum((part.astype(F32) - average) * scale + shift, 0.0) * mask
        field[x + 1, y + 1] = part.astype(BF16)

    zero = jnp.zeros((channels, depth), F32)
    sums = Sums(zero, zero)

    def emit(x, y, value):
        value = (value * wide_masks[x // BRICK + 1, y // BRICK + 1][:1]).astype(BF16)
        second_out[x, y] = value
        sums.add(value)

    groups = [(x, y) for x in range(0, extent_x, 2) for y in range(0, extent_y, 2)]
    convolve_groups(
        groups, lambda x, y: field[x + 1, y + 1], band, channels, depth, emit, activate
    )
    counts = jnp.zeros((BRICK, depth), F32)
    for i in range(bx):
        for j in range(by):
            counts = counts + wide_masks[1 + i, 1 + j] * float(BRICK)
    send_stats(stats, channels, sums.sums, sums.squares, counts)


def last_kernel(dims, second_out, wide_masks, received, params, own, result, turned, ready, sent):
    channels, extent_x, extent_y, depth, bx, by = dims
    average, scale = affine(received, params[2], channels, depth)
    shift = params[3]
    copies = []
    for x in range(extent_x):
        for j in range(by):
            mask = wide_masks[x // BRICK + 1, j + 1][:1]
            for y in range(BRICK):
                at = j * BRICK + y
                part = second_out[x, at].astype(F32)
                part = (part - average) * scale + shift + own[x, at].astype(F32)
                part = jnp.maximum(part, 0.0) * mask
                turned[x % 2, pl.ds(y, channels, stride=BRICK), :] = part
            ready[:, x, j * BRICK : (j + 1) * BRICK, :] = (
                turned[x % 2].reshape(channels, BRICK, depth).astype(BF16)
            )
        if x % 2 == 1:
            copy = pltpu.make_async_copy(
                ready.at[:, x - 1 : x + 1], result.at[:, x - 1 : x + 1], sent.at[x // 2]
            )
            copy.start()
            copies.append(copy)
    for copy in copies:
        copy.wait()


def per_device(
    features,
    brick_mask,
    conv_first,
    conv_second,
    gain_first,
    shift_first,
    gain_second,
    shift_second,
):
    channels, extent_x, extent_y, depth = features.shape
    bx, by, bz = brick_mask.shape
    dims = (channels, extent_x, extent_y, depth, bx, by)
    devices = lax.axis_size(AXES)
    shape = jax.ShapeDtypeStruct

    x_rows = HALO * extent_y * channels + BRICK * by
    y_rows = HALO * extent_x * channels + BRICK * bx
    c_rows = 2 * HALO * HALO * channels + 2 * BRICK
    turned = pltpu.VMEM((2, channels * BRICK, depth), F32)
    masks, x_even, x_odd = call(
        functools.partial(edge_kernel, dims),
        (
            shape((bx * by, BRICK, depth), F32),
            shape((x_rows, depth), BF16),
            shape((x_rows, depth), BF16),
        ),
        (
            pltpu.with_memory_space_constraint(features, pltpu.HBM),
            pltpu.with_memory_space_constraint(brick_mask.reshape(bx * by, bz), pltpu.HBM),
        ),
        scratch=[
            pltpu.VMEM((2, channels, HALO, extent_y, depth), BF16),
            pltpu.VMEM((bx * by, bz), jnp.int32),
            turned,
            pltpu.VMEM((2, HALO * extent_y * channels, depth), BF16),
            pltpu.SemaphoreType.DMA((2,)),
            pltpu.SemaphoreType.DMA,
        ],
        far=(0, 1),
    )
    x_pair = swap(x_even, x_odd, "region")
    own, y_even, y_odd = call(
        functools.partial(gather_kernel, dims),
        (
            shape((extent_x, extent_y, channels, depth), BF16),
            shape((y_rows, depth), BF16),
            shape((y_rows, depth), BF16),
        ),
        (features, masks),
        scratch=[turned],
    )
    y_pair = swap(y_even, y_odd, "strip")
    corners = call(
        functools.partial(corner_kernel, dims),
        (shape((c_rows, depth), BF16), shape((c_rows, depth), BF16)),
        x_pair,
    )
    c_pair = swap(*corners, "strip")

    band_shape = shape((12 * channels, 16 * channels), BF16)
    first_band, second_band, params = call(
        prepare_kernel,
        (band_shape, band_shape, shape((4, channels, depth), F32)),
        (
            conv_first,
            conv_second,
            jnp.stack([gain_first, shift_first, gain_second, shift_second]),
        ),
    )
    wide_shape = (extent_x + 2, extent_y + 2, channels, depth)
    first_out, partial = call(
        functools.partial(first_kernel, dims),
        (shape(wide_shape, BF16), shape((2, channels, depth), F32)),
        (own, masks, *x_pair, *y_pair, first_band),
    )
    corner_out, wide_masks, sent = call(
        functools.partial(finish_kernel, dims),
        (
            shape((4, 4, channels, depth), BF16),
            shape((bx + 2, by + 2, BRICK, depth), F32),
            shape((devices, 128), F32),
        ),
        (own, masks, *x_pair, *y_pair, *c_pair, first_band, partial),
    )
    received = lax.all_to_all(sent, AXES, 0, 0, tiled=True)
    second_out, sent = call(
        functools.partial(second_kernel, dims),
        (
            shape((extent_x, extent_y, channels, depth), BF16),
            shape((devices, 128), F32),
        ),
        (first_out, corner_out, wide_masks, received, params, second_band),
        scratch=[pltpu.VMEM(wide_shape, BF16)],
    )
    received = lax.all_to_all(sent, AXES, 0, 0, tiled=True)
    return call(
        functools.partial(last_kernel, dims),
        shape(features.shape, BF16),
        (second_out, wide_masks, received, params, own),
        scratch=[
            turned,
            pltpu.VMEM(features.shape, BF16),
            pltpu.SemaphoreType.DMA((extent_x // 2,)),
        ],
        far_out=True,
    )


def solution(mesh):
    in_specs = (
        P(None, "region", "strip", None),
        P("region", "strip", None),
        P(),
        P(),
        P(),
        P(),
        P(),
        P(),
    )
    out_specs = P(None, "region", "strip", None)
    return jax.shard_map(
        per_device, mesh=mesh, in_specs=in_specs, out_specs=out_specs, check_vma=False
    )
```

```python
import functools

import jax
import jax.numpy as jnp
from jax import lax
from jax.experimental import pallas as pl
from jax.experimental.pallas import tpu as pltpu
from jax.sharding import PartitionSpec as P


BRICK = 8
EPSILON = 1e-05
HALO = 2
PART = 16
AXES = ("region", "strip")
F32 = jnp.float32
BF16 = jnp.bfloat16


def even_pairs(count):
    return [(i, i ^ 1) for i in range(count) if (i ^ 1) < count]


def odd_pairs(count):
    pairs = [(i, i + 1) for i in range(1, count - 1, 2)]
    return pairs + [(b, a) for a, b in pairs]


def swap(even, odd, axis):
    count = lax.axis_size(axis)
    even = lax.ppermute(even, axis, even_pairs(count))
    odd = lax.ppermute(odd, axis, odd_pairs(count))
    return even, odd


def call(body, outs, ins, scratch=(), far=(), far_out=False):
    def space(is_far):
        return pl.BlockSpec(memory_space=pltpu.HBM if is_far else pltpu.VMEM)

    return pl.pallas_call(
        body,
        out_shape=outs,
        in_specs=[space(i in far) for i in range(len(ins))],
        out_specs=jax.tree.map(lambda _: space(far_out), outs),
        scratch_shapes=list(scratch),
        compiler_params=pltpu.CompilerParams(vmem_limit_bytes=16 << 20),
        cost_estimate=pl.CostEstimate(
            flops=0,
            transcendentals=0,
            bytes_accessed=sum(a.size * a.dtype.itemsize for a in ins),
        ),
    )(*ins)


def is_even(axis):
    return lax.rem(lax.axis_index(axis), 2) == 0


def brick_rows(bricks, depth):
    count = bricks.shape[1]
    at = lax.broadcasted_iota(jnp.int32, (count, depth), 0)
    voxel = lax.broadcasted_iota(jnp.int32, (count, depth), 1)
    spread = (voxel // BRICK == at).astype(F32)
    return jnp.dot(bricks, spread, preferred_element_type=F32)


def sides(even_place, even, odd):
    return ((even, jnp.where(even_place, 0, 1)), (odd, jnp.where(even_place, 1, 0)))


def turn(dims, raw, x, raw_x, masks, turned, keep):
    channels, _, _, depth, _, by = dims
    for j in range(by):
        part = raw[:, raw_x, j * BRICK : (j + 1) * BRICK, :].astype(F32)
        part = part * masks[x // BRICK * by + j][None]
        turned[x % 2] = part.reshape(channels * BRICK, depth)
        for y in range(BRICK):
            value = turned[x % 2, pl.ds(y, channels, stride=BRICK), :]
            keep(j * BRICK + y, value.astype(BF16))


def edge_kernel(dims, features, bricks, *refs):
    masks, even, odd, raw, flags, turned, edge, arrived, flags_arrived = refs
    channels, extent_x, extent_y, depth, bx, by = dims
    flag_copy = pltpu.make_async_copy(bricks, flags, flags_arrived)
    flag_copy.start()
    copies = []
    for side in range(2):
        start = side * (extent_x - HALO)
        copy = pltpu.make_async_copy(
            features.at[:, start : start + HALO], raw.at[side], arrived.at[side]
        )
        copy.start()
        copies.append(copy)
    flag_copy.wait()
    rows = brick_rows(flags[...].astype(F32), depth)
    for i in range(bx * by):
        masks[i] = jnp.broadcast_to(rows[i : i + 1], (BRICK, depth))
    for side in range(2):
        copies[side].wait()
        for i in range(HALO):

            def keep(y, value):
                at = (i * extent_y + y) * channels
                edge[1 - side, at : at + channels, :] = value

            turn(dims, raw.at[side], side * (extent_x - HALO) + i, i, masks, turned, keep)
    rows = HALO * extent_y * channels
    for out, low in sides(is_even("region"), even, odd):
        out[:rows, :] = edge[low]
        for j in range(by):
            tile = masks[jnp.where(low == 1, 0, bx - 1) * by + j]
            out[rows + BRICK * j : rows + BRICK * (j + 1), :] = tile.astype(BF16)


def gather_kernel(dims, features, masks, own, even, odd, turned):
    channels, extent_x, extent_y, _, bx, by = dims
    for x in range(extent_x):

        def keep(y, value):
            own[x, y] = value

        turn(dims, features, x, x, masks, turned, keep)
    for out, low in sides(is_even("strip"), even, odd):
        start = jnp.where(low == 1, 0, extent_y - HALO)
        for x in range(extent_x):
            for j in range(HALO):
                at = (x * HALO + j) * channels
                out[at : at + channels, :] = own[x, start + j]
        base = extent_x * HALO * channels
        for i in range(bx):
            tile = masks[i * by + jnp.where(low == 1, 0, by - 1)]
            out[base + BRICK * i : base + BRICK * (i + 1), :] = tile.astype(BF16)


def corner_kernel(dims, x_even, x_odd, even, odd):
    channels, _, extent_y, _, _, by = dims
    first_x = is_even("region")
    base = HALO * extent_y * channels
    for out, low in sides(is_even("strip"), even, odd):
        start = jnp.where(low == 1, 0, extent_y - HALO)
        brick = jnp.where(low == 1, 0, by - 1)
        half = HALO * HALO * channels
        for i in range(HALO):
            for j in range(HALO):
                at = pl.multiple_of((i * extent_y + start + j) * channels, channels)
                a = x_even[pl.ds(at, channels), :]
                b = x_odd[pl.ds(at, channels), :]
                to = (i * HALO + j) * channels
                out[to : to + channels, :] = jnp.where(first_x, b, a)
                out[half + to : half + to + channels, :] = jnp.where(first_x, a, b)
        at = pl.multiple_of(base + brick * BRICK, BRICK)
        a = x_even[pl.ds(at, BRICK), :].astype(F32)
        b = x_odd[pl.ds(at, BRICK), :].astype(F32)
        tiles = (jnp.where(first_x, b, a), jnp.where(first_x, a, b))
        out[2 * half : 2 * half + 2 * BRICK, :] = jnp.concatenate(tiles, axis=0).astype(BF16)


def prepare_kernel(weights_first, weights_second, rows, first_band, second_band, params):
    for weights, band in ((weights_first, first_band), (weights_second, second_band)):
        fan_in, fan_out = weights.shape[3:]
        wide = 4 * fan_in
        blank = jnp.zeros((fan_out, wide), BF16)
        for dz in range(3):
            pieces = []
            for dx in range(3):
                part = jnp.concatenate([weights[dx, dy, dz].astype(F32) for dy in range(3)], axis=0)
                part = jnp.concatenate([part, jnp.zeros((fan_in, fan_out), F32)], axis=0)
                part = jnp.concatenate([part, jnp.zeros((wide, 128 - fan_out), F32)], axis=1)
                part = jnp.transpose(part)[:fan_out]
                pieces.append((part.astype(BF16), pltpu.roll(part, fan_in, 1).astype(BF16)))
            for x in range(2):
                for y in range(2):
                    at = ((dz * 2 + x) * 2 + y) * fan_out
                    for i in range(4):
                        piece = pieces[i - x][y] if 0 <= i - x < 3 else blank
                        band[at : at + fan_out, i * wide : (i + 1) * wide] = piece
    channels = rows.shape[1]
    for i in range(4):
        row = jnp.concatenate([rows[i : i + 1, :], jnp.zeros((1, 128 - channels), F32)], axis=1)
        params[i] = jnp.transpose(jnp.broadcast_to(row, (128, 128)))[:channels]


def window_of(group):
    return [(group[0] + a - 1, group[1] + b - 1) for a in range(4) for b in range(4)]


def convolve_groups(groups, column, band, channels, depth, emit, ready=None):
    pairs = [groups[i : i + 2] for i in range(0, len(groups), 2)]

    def prepare(i):
        if ready is not None and i < len(pairs):
            for group in pairs[i]:
                for x, y in window_of(group):
                    ready(x, y)

    def value_of(total, n, a, b):
        before, here, after = (
            total[
                ((dz * 2 + a) * 2 + b) * channels : ((dz * 2 + a) * 2 + b + 1) * channels,
                n * depth : (n + 1) * depth,
            ]
            for dz in range(3)
        )
        before = jnp.where(at_start, 0.0, pltpu.roll(before, 1, 1))
        after = jnp.where(at_end, 0.0, pltpu.roll(after, depth - 1, 1))
        return here + before + after

    prepare(0)
    lane = lax.broadcasted_iota(jnp.int32, (channels, depth), 1)
    at_start, at_end = lane == 0, lane == depth - 1
    for i, pair in enumerate(pairs):
        windows = [jnp.concatenate([column(*at) for at in window_of(g)], axis=0) for g in pair]
        window = jnp.concatenate(windows, axis=1) if len(windows) > 1 else windows[0]
        total = jnp.dot(band[...], window, preferred_element_type=F32)
        prepare(i + 1)
        for n, (x, y) in enumerate(pair):
            for a in range(2):
                for b in range(2):
                    emit(x + a, y + b, functools.partial(value_of, total, n, a, b))


def send_stats(out, channels, sums, squares, counts):
    depth = sums.shape[1]
    rest = jnp.zeros((128 - 2 * channels - counts.shape[0], depth), F32)
    table = jnp.concatenate([sums, squares, counts, rest], axis=0)
    row = jnp.sum(jnp.transpose(table), axis=0, keepdims=True)
    out[...] = jnp.broadcast_to(row, out.shape)


def affine(stats, gain, shift, channels):
    row = jnp.sum(stats[...], axis=0, keepdims=True)
    table = jnp.transpose(jnp.broadcast_to(row, (128, 128)))
    total = jnp.sum(table[2 * channels : 2 * channels + BRICK], axis=0, keepdims=True)
    average = table[:channels] / total
    variance = table[channels : 2 * channels] / total - average * average
    scale = lax.rsqrt(variance + EPSILON) * gain
    return scale, shift - average * scale


class Edges:
    def __init__(self, dims, own, masks, x_pair, y_pair, corner_pair=None):
        self.dims = dims
        self.own, self.masks = own, masks
        self.x_pair, self.y_pair, self.corner_pair = x_pair, y_pair, corner_pair
        self.first_x, self.first_y = is_even("region"), is_even("strip")

    def pick(self, pair, first, low, at, rows):
        even, odd = (ref[at : at + rows, :] for ref in pair)
        if rows == BRICK:
            even, odd = even.astype(F32), odd.astype(F32)
        return jnp.where(first, odd, even) if low else jnp.where(first, even, odd)

    def column(self, x, y):
        channels, extent_x, extent_y = self.dims[:3]
        inside_x, inside_y = 0 <= x < extent_x, 0 <= y < extent_y
        if inside_x and inside_y:
            return self.own[x, y]
        i = x + HALO if x < 0 else x - extent_x
        j = y + HALO if y < 0 else y - extent_y
        if inside_y:
            at = (i * extent_y + y) * channels
            return self.pick(self.x_pair, self.first_x, x < 0, at, channels)
        if inside_x:
            at = (x * HALO + j) * channels
            return self.pick(self.y_pair, self.first_y, y < 0, at, channels)
        at = ((int(x > 0) * HALO + i) * HALO + j) * channels
        return self.pick(self.corner_pair, self.first_y, y < 0, at, channels)

    def mask(self, i, j):
        channels, extent_x, extent_y, _, bx, by = self.dims
        inside_x, inside_y = 0 <= i < bx, 0 <= j < by
        if inside_x and inside_y:
            return self.masks[i * by + j]
        if inside_y:
            at = HALO * extent_y * channels + BRICK * j
            tile = self.pick(self.x_pair, self.first_x, i < 0, at, BRICK)
        elif inside_x:
            at = HALO * extent_x * channels + BRICK * i
            tile = self.pick(self.y_pair, self.first_y, j < 0, at, BRICK)
        else:
            at = 2 * HALO * HALO * channels + BRICK * int(i > 0)
            tile = self.pick(self.corner_pair, self.first_y, j < 0, at, BRICK)
        return tile


class Sums:
    def __init__(self, sums, squares):
        self.sums, self.squares = sums, squares

    def add(self, value):
        value = value.astype(F32)
        self.sums = self.sums + value
        self.squares = self.squares + value * value


def ring_groups(extent_x, extent_y):
    far = (extent_x - 1, extent_y - 1)
    groups = [(x, y) for x in range(-1, extent_x, 2) for y in range(-1, extent_y, 2)]
    corners = [g for g in groups if g[0] in (-1, far[0]) and g[1] in (-1, far[1])]
    return [g for g in groups if g not in corners], corners


def first_kernel(dims, own, masks, x_even, x_odd, y_even, y_odd, band, first_out, partial):
    channels, extent_x, extent_y, depth, _, _ = dims
    edges = Edges(dims, own, masks, (x_even, x_odd), (y_even, y_odd))
    found = {}
    zero = jnp.zeros((channels, depth), F32)
    sums = Sums(zero, zero)

    def emit(x, y, value):
        brick = (x // BRICK, y // BRICK)
        if brick not in found:
            found[brick] = edges.mask(*brick)[:1]
        value = (value() * found[brick]).astype(BF16)
        first_out[x + 1, y + 1] = value
        if 0 <= x < extent_x and 0 <= y < extent_y:
            sums.add(value)

    groups = ring_groups(extent_x, extent_y)[0]
    convolve_groups(groups, edges.column, band, channels, depth, emit)
    partial[0] = sums.sums
    partial[1] = sums.squares


def finish_kernel(dims, own, masks, *refs):
    x_even, x_odd, y_even, y_odd, c_even, c_odd, band, partial, corner_out, wide_masks, stats = refs
    channels, extent_x, extent_y, depth, bx, by = dims
    edges = Edges(dims, own, masks, (x_even, x_odd), (y_even, y_odd), (c_even, c_odd))
    counts = jnp.zeros((BRICK, depth), F32)
    for i in range(-1, bx + 1):
        for j in range(-1, by + 1):
            tile = edges.mask(i, j)
            wide_masks[i + 1, j + 1] = tile
            if 0 <= i < bx and 0 <= j < by:
                counts = counts + tile * float(BRICK)
    sums = Sums(partial[0], partial[1])

    outputs = []
    groups = ring_groups(extent_x, extent_y)[1]
    convolve_groups(groups, edges.column, band, channels, depth, lambda *it: outputs.append(it))

    def put(x, y, value):
        value = (value() * edges.mask(x // BRICK, y // BRICK)[:1]).astype(BF16)
        side_x, side_y = int(x >= extent_x - 1), int(y >= extent_y - 1)
        i = x - (extent_x - 1 if side_x else -1)
        j = y - (extent_y - 1 if side_y else -1)
        corner_out[2 * side_x + i, 2 * side_y + j] = value
        return value

    def is_own(x, y):
        return 0 <= x < extent_x and 0 <= y < extent_y

    for x, y, value in outputs:
        if is_own(x, y):
            sums.add(put(x, y, value))
    send_stats(stats, channels, sums.sums, sums.squares, counts)
    for x, y, value in outputs:
        if not is_own(x, y):
            put(x, y, value)


def second_kernel(dims, *refs):
    first_out, corner_out, wide_masks, received, params, band, second_out, stats, field = refs
    channels, extent_x, extent_y, depth, bx, by = dims
    scale, offset = affine(received, params[0], params[1], channels)
    edge_x, edge_y = (0, 1, extent_x, extent_x + 1), (0, 1, extent_y, extent_y + 1)
    done = set()

    def activate(x, y):
        if (x, y) in done:
            return
        done.add((x, y))
        if x + 1 in edge_x and y + 1 in edge_y:
            part = corner_out[edge_x.index(x + 1), edge_y.index(y + 1)]
        else:
            part = first_out[x + 1, y + 1]
        mask = wide_masks[x // BRICK + 1, y // BRICK + 1][:1]
        part = jnp.maximum(part.astype(F32) * scale + offset, 0.0) * mask
        field[x + 1, y + 1] = part.astype(BF16)

    zero = jnp.zeros((channels, depth), F32)
    sums = Sums(zero, zero)

    def emit(x, y, value):
        value = (value() * wide_masks[x // BRICK + 1, y // BRICK + 1][:1]).astype(BF16)
        second_out[x, y] = value
        sums.add(value)

    groups = [(x, y) for x in range(0, extent_x, 2) for y in range(0, extent_y, 2)]
    convolve_groups(
        groups, lambda x, y: field[x + 1, y + 1], band, channels, depth, emit, activate
    )
    counts = jnp.zeros((BRICK, depth), F32)
    for i in range(bx):
        for j in range(by):
            counts = counts + wide_masks[1 + i, 1 + j] * float(BRICK)
    send_stats(stats, channels, sums.sums, sums.squares, counts)


def last_kernel(dims, second_out, wide_masks, received, params, own, result, turned, ready, sent):
    channels, extent_x, _, depth, _, by = dims
    scale, offset = affine(received, params[2], params[3], channels)
    copies = []
    for start in range(0, channels, PART):
        rows = slice(start, start + PART)
        for x in range(extent_x):
            for j in range(by):
                mask = wide_masks[x // BRICK + 1, j + 1][:1]
                for y in range(BRICK):
                    at = j * BRICK + y
                    part = second_out[x, at, rows].astype(F32) * scale[rows] + offset[rows]
                    part = jnp.maximum(part + own[x, at, rows].astype(F32), 0.0) * mask
                    turned[x % 2, pl.ds(y, PART, stride=BRICK), :] = part
                ready[rows, x, j * BRICK : (j + 1) * BRICK, :] = (
                    turned[x % 2, : PART * BRICK].reshape(PART, BRICK, depth).astype(BF16)
                )
        copy = pltpu.make_async_copy(ready.at[rows], result.at[rows], sent.at[start // PART])
        copy.start()
        copies.append(copy)
    for copy in copies:
        copy.wait()


def per_device(
    features,
    brick_mask,
    conv_first,
    conv_second,
    gain_first,
    shift_first,
    gain_second,
    shift_second,
):
    channels, extent_x, extent_y, depth = features.shape
    bx, by, bz = brick_mask.shape
    dims = (channels, extent_x, extent_y, depth, bx, by)
    devices = lax.axis_size(AXES)
    shape = jax.ShapeDtypeStruct

    x_rows = HALO * extent_y * channels + BRICK * by
    y_rows = HALO * extent_x * channels + BRICK * bx
    c_rows = 2 * HALO * HALO * channels + 2 * BRICK
    turned = pltpu.VMEM((2, channels * BRICK, depth), F32)
    masks, x_even, x_odd = call(
        functools.partial(edge_kernel, dims),
        (
            shape((bx * by, BRICK, depth), F32),
            shape((x_rows, depth), BF16),
            shape((x_rows, depth), BF16),
        ),
        (
            pltpu.with_memory_space_constraint(features, pltpu.HBM),
            pltpu.with_memory_space_constraint(brick_mask.reshape(bx * by, bz), pltpu.HBM),
        ),
        scratch=[
            pltpu.VMEM((2, channels, HALO, extent_y, depth), BF16),
            pltpu.VMEM((bx * by, bz), jnp.int32),
            turned,
            pltpu.VMEM((2, HALO * extent_y * channels, depth), BF16),
            pltpu.SemaphoreType.DMA((2,)),
            pltpu.SemaphoreType.DMA,
        ],
        far=(0, 1),
    )
    x_pair = swap(x_even, x_odd, "region")
    own, y_even, y_odd = call(
        functools.partial(gather_kernel, dims),
        (
            shape((extent_x, extent_y, channels, depth), BF16),
            shape((y_rows, depth), BF16),
            shape((y_rows, depth), BF16),
        ),
        (features, masks),
        scratch=[turned],
    )
    y_pair = swap(y_even, y_odd, "strip")
    corners = call(
        functools.partial(corner_kernel, dims),
        (shape((c_rows, depth), BF16), shape((c_rows, depth), BF16)),
        x_pair,
    )
    c_pair = swap(*corners, "strip")

    band_shape = shape((12 * channels, 16 * channels), BF16)
    first_band, second_band, params = call(
        prepare_kernel,
        (band_shape, band_shape, shape((4, channels, depth), F32)),
        (
            conv_first,
            conv_second,
            jnp.stack([gain_first, shift_first, gain_second, shift_second]),
        ),
    )
    wide_shape = (extent_x + 2, extent_y + 2, channels, depth)
    first_out, partial = call(
        functools.partial(first_kernel, dims),
        (shape(wide_shape, BF16), shape((2, channels, depth), F32)),
        (own, masks, *x_pair, *y_pair, first_band),
    )
    corner_out, wide_masks, sent = call(
        functools.partial(finish_kernel, dims),
        (
            shape((4, 4, channels, depth), BF16),
            shape((bx + 2, by + 2, BRICK, depth), F32),
            shape((devices, 128), F32),
        ),
        (own, masks, *x_pair, *y_pair, *c_pair, first_band, partial),
    )
    received = lax.all_to_all(sent, AXES, 0, 0, tiled=True)
    second_out, sent = call(
        functools.partial(second_kernel, dims),
        (
            shape((extent_x, extent_y, channels, depth), BF16),
            shape((devices, 128), F32),
        ),
        (first_out, corner_out, wide_masks, received, params, second_band),
        scratch=[pltpu.VMEM(wide_shape, BF16)],
    )
    received = lax.all_to_all(sent, AXES, 0, 0, tiled=True)
    return call(
        functools.partial(last_kernel, dims),
        shape(features.shape, BF16),
        (second_out, wide_masks, received, params, own),
        scratch=[
            turned,
            pltpu.VMEM(features.shape, BF16),
            pltpu.SemaphoreType.DMA((channels // PART,)),
        ],
        far_out=True,
    )


def solution(mesh):
    in_specs = (
        P(None, "region", "strip", None),
        P("region", "strip", None),
        P(),
        P(),
        P(),
        P(),
        P(),
        P(),
    )
    out_specs = P(None, "region", "strip", None)
    return jax.shard_map(
        per_device, mesh=mesh, in_specs=in_specs, out_specs=out_specs, check_vma=False
    )
```

```python
import functools

import jax
import jax.numpy as jnp
from jax import lax
from jax.experimental import pallas as pl
from jax.experimental.pallas import tpu as pltpu
from jax.sharding import PartitionSpec as P


BRICK = 8
EPSILON = 1e-05
HALO = 2
PART = 16
AXES = ("region", "strip")
F32 = jnp.float32
BF16 = jnp.bfloat16


def even_pairs(count):
    return [(i, i ^ 1) for i in range(count) if (i ^ 1) < count]


def odd_pairs(count):
    pairs = [(i, i + 1) for i in range(1, count - 1, 2)]
    return pairs + [(b, a) for a, b in pairs]


def swap(even, odd, axis):
    count = lax.axis_size(axis)
    even = lax.ppermute(even, axis, even_pairs(count))
    odd = lax.ppermute(odd, axis, odd_pairs(count))
    return even, odd


def call(body, outs, ins, scratch=(), far=(), far_out=False):
    def space(is_far):
        return pl.BlockSpec(memory_space=pltpu.HBM if is_far else pltpu.VMEM)

    return pl.pallas_call(
        body,
        out_shape=outs,
        in_specs=[space(i in far) for i in range(len(ins))],
        out_specs=jax.tree.map(lambda _: space(far_out), outs),
        scratch_shapes=list(scratch),
        compiler_params=pltpu.CompilerParams(vmem_limit_bytes=16 << 20),
        cost_estimate=pl.CostEstimate(
            flops=0,
            transcendentals=0,
            bytes_accessed=sum(a.size * a.dtype.itemsize for a in ins),
        ),
    )(*ins)


def is_even(axis):
    return lax.rem(lax.axis_index(axis), 2) == 0


def brick_rows(bricks, depth):
    count = bricks.shape[1]
    at = lax.broadcasted_iota(jnp.int32, (count, depth), 0)
    voxel = lax.broadcasted_iota(jnp.int32, (count, depth), 1)
    spread = (voxel // BRICK == at).astype(F32)
    return jnp.dot(bricks, spread, preferred_element_type=F32)


def sides(even_place, even, odd):
    return ((even, jnp.where(even_place, 0, 1)), (odd, jnp.where(even_place, 1, 0)))


def turn(dims, raw, x, raw_x, masks, turned, keep):
    channels, _, _, depth, _, by = dims
    for j in range(by):
        part = raw[:, raw_x, j * BRICK : (j + 1) * BRICK, :].astype(F32)
        part = part * masks[x // BRICK * by + j][None]
        turned[x % 2] = part.reshape(channels * BRICK, depth)
        for y in range(BRICK):
            value = turned[x % 2, pl.ds(y, channels, stride=BRICK), :]
            keep(j * BRICK + y, value.astype(BF16))


def edge_kernel(dims, features, bricks, *refs):
    masks, even, odd, raw, flags, turned, edge, arrived, flags_arrived = refs
    channels, extent_x, extent_y, depth, bx, by = dims
    flag_copy = pltpu.make_async_copy(bricks, flags, flags_arrived)
    flag_copy.start()
    copies = []
    for side in range(2):
        start = side * (extent_x - HALO)
        copy = pltpu.make_async_copy(
            features.at[:, start : start + HALO], raw.at[side], arrived.at[side]
        )
        copy.start()
        copies.append(copy)
    flag_copy.wait()
    rows = brick_rows(flags[...].astype(F32), depth)
    for i in range(bx * by):
        masks[i] = jnp.broadcast_to(rows[i : i + 1], (BRICK, depth))
    for side in range(2):
        copies[side].wait()
        for i in range(HALO):

            def keep(y, value):
                at = (i * extent_y + y) * channels
                edge[1 - side, at : at + channels, :] = value

            turn(dims, raw.at[side], side * (extent_x - HALO) + i, i, masks, turned, keep)
    rows = HALO * extent_y * channels
    for out, low in sides(is_even("region"), even, odd):
        out[:rows, :] = edge[low]
        for j in range(by):
            tile = masks[jnp.where(low == 1, 0, bx - 1) * by + j]
            out[rows + BRICK * j : rows + BRICK * (j + 1), :] = tile.astype(BF16)


def gather_kernel(dims, features, masks, own, even, odd, turned):
    channels, extent_x, extent_y, _, bx, by = dims
    for x in range(extent_x):

        def keep(y, value):
            own[x, y] = value

        turn(dims, features, x, x, masks, turned, keep)
    for out, low in sides(is_even("strip"), even, odd):
        start = jnp.where(low == 1, 0, extent_y - HALO)
        for x in range(extent_x):
            for j in range(HALO):
                at = (x * HALO + j) * channels
                out[at : at + channels, :] = own[x, start + j]
        base = extent_x * HALO * channels
        for i in range(bx):
            tile = masks[i * by + jnp.where(low == 1, 0, by - 1)]
            out[base + BRICK * i : base + BRICK * (i + 1), :] = tile.astype(BF16)


def corner_kernel(dims, x_even, x_odd, even, odd):
    channels, _, extent_y, _, _, by = dims
    first_x = is_even("region")
    base = HALO * extent_y * channels
    for out, low in sides(is_even("strip"), even, odd):
        start = jnp.where(low == 1, 0, extent_y - HALO)
        brick = jnp.where(low == 1, 0, by - 1)
        half = HALO * HALO * channels
        for i in range(HALO):
            for j in range(HALO):
                at = pl.multiple_of((i * extent_y + start + j) * channels, channels)
                a = x_even[pl.ds(at, channels), :]
                b = x_odd[pl.ds(at, channels), :]
                to = (i * HALO + j) * channels
                out[to : to + channels, :] = jnp.where(first_x, b, a)
                out[half + to : half + to + channels, :] = jnp.where(first_x, a, b)
        at = pl.multiple_of(base + brick * BRICK, BRICK)
        a = x_even[pl.ds(at, BRICK), :].astype(F32)
        b = x_odd[pl.ds(at, BRICK), :].astype(F32)
        tiles = (jnp.where(first_x, b, a), jnp.where(first_x, a, b))
        out[2 * half : 2 * half + 2 * BRICK, :] = jnp.concatenate(tiles, axis=0).astype(BF16)


def prepare_kernel(weights_first, weights_second, rows, first_band, second_band, params):
    for weights, band in ((weights_first, first_band), (weights_second, second_band)):
        fan_in, fan_out = weights.shape[3:]
        wide = 4 * fan_in
        blank = jnp.zeros((fan_out, wide), BF16)
        for dz in range(3):
            pieces = []
            for dx in range(3):
                part = jnp.concatenate([weights[dx, dy, dz].astype(F32) for dy in range(3)], axis=0)
                part = jnp.concatenate([part, jnp.zeros((fan_in, fan_out), F32)], axis=0)
                part = jnp.concatenate([part, jnp.zeros((wide, 128 - fan_out), F32)], axis=1)
                part = jnp.transpose(part)[:fan_out]
                pieces.append((part.astype(BF16), pltpu.roll(part, fan_in, 1).astype(BF16)))
            for x in range(2):
                for y in range(2):
                    at = ((dz * 2 + x) * 2 + y) * fan_out
                    for i in range(4):
                        piece = pieces[i - x][y] if 0 <= i - x < 3 else blank
                        band[at : at + fan_out, i * wide : (i + 1) * wide] = piece
    channels = rows.shape[1]
    for i in range(4):
        row = jnp.concatenate([rows[i : i + 1, :], jnp.zeros((1, 128 - channels), F32)], axis=1)
        params[i] = jnp.transpose(jnp.broadcast_to(row, (128, 128)))[:channels]


def window_of(group):
    return [(group[0] + a - 1, group[1] + b - 1) for a in range(4) for b in range(4)]


def convolve_groups(groups, column, band, channels, depth, emit, ready=None):
    pairs = [groups[i : i + 2] for i in range(0, len(groups), 2)]

    def prepare(i):
        if ready is not None and i < len(pairs):
            for group in pairs[i]:
                for x, y in window_of(group):
                    ready(x, y)

    def rows_of(a):
        wide = 2 * channels
        parts = [band[(dz * 2 + a) * wide : (dz * 2 + a + 1) * wide, :] for dz in range(3)]
        return jnp.concatenate(parts, axis=0)

    def value_of(total, n, b):
        before, here, after = (
            total[(2 * dz + b) * channels : (2 * dz + b + 1) * channels, n * depth : (n + 1) * depth]
            for dz in range(3)
        )
        before = jnp.where(at_start, 0.0, pltpu.roll(before, 1, 1))
        after = jnp.where(at_end, 0.0, pltpu.roll(after, depth - 1, 1))
        return here + before + after

    lane = lax.broadcasted_iota(jnp.int32, (channels, depth), 1)
    at_start, at_end = lane == 0, lane == depth - 1
    prepare(0)
    for i, pair in enumerate(pairs):
        windows = [jnp.concatenate([column(*at) for at in window_of(g)], axis=0) for g in pair]
        window = jnp.concatenate(windows, axis=1) if len(windows) > 1 else windows[0]
        prepare(i + 1)
        for a in range(2):
            total = jnp.dot(rows_of(a), window, preferred_element_type=F32)
            for n, (x, y) in enumerate(pair):
                for b in range(2):
                    emit(x + a, y + b, functools.partial(value_of, total, n, b))


def send_stats(out, channels, sums, squares, counts):
    depth = sums.shape[1]
    rest = jnp.zeros((128 - 2 * channels - counts.shape[0], depth), F32)
    table = jnp.concatenate([sums, squares, counts, rest], axis=0)
    row = jnp.sum(jnp.transpose(table), axis=0, keepdims=True)
    out[...] = jnp.broadcast_to(row, out.shape)


def affine(stats, gain, shift, channels):
    row = jnp.sum(stats[...], axis=0, keepdims=True)
    table = jnp.transpose(jnp.broadcast_to(row, (128, 128)))
    total = jnp.sum(table[2 * channels : 2 * channels + BRICK], axis=0, keepdims=True)
    average = table[:channels] / total
    variance = table[channels : 2 * channels] / total - average * average
    scale = lax.rsqrt(variance + EPSILON) * gain
    return scale, shift - average * scale


class Edges:
    def __init__(self, dims, own, masks, x_pair, y_pair, corner_pair=None):
        self.dims = dims
        self.own, self.masks = own, masks
        self.x_pair, self.y_pair, self.corner_pair = x_pair, y_pair, corner_pair
        self.first_x, self.first_y = is_even("region"), is_even("strip")

    def pick(self, pair, first, low, at, rows):
        even, odd = (ref[at : at + rows, :] for ref in pair)
        if rows == BRICK:
            even, odd = even.astype(F32), odd.astype(F32)
        return jnp.where(first, odd, even) if low else jnp.where(first, even, odd)

    def column(self, x, y):
        channels, extent_x, extent_y = self.dims[:3]
        inside_x, inside_y = 0 <= x < extent_x, 0 <= y < extent_y
        if inside_x and inside_y:
            return self.own[x, y]
        i = x + HALO if x < 0 else x - extent_x
        j = y + HALO if y < 0 else y - extent_y
        if inside_y:
            at = (i * extent_y + y) * channels
            return self.pick(self.x_pair, self.first_x, x < 0, at, channels)
        if inside_x:
            at = (x * HALO + j) * channels
            return self.pick(self.y_pair, self.first_y, y < 0, at, channels)
        at = ((int(x > 0) * HALO + i) * HALO + j) * channels
        return self.pick(self.corner_pair, self.first_y, y < 0, at, channels)

    def mask(self, i, j):
        channels, extent_x, extent_y, _, bx, by = self.dims
        inside_x, inside_y = 0 <= i < bx, 0 <= j < by
        if inside_x and inside_y:
            return self.masks[i * by + j]
        if inside_y:
            at = HALO * extent_y * channels + BRICK * j
            tile = self.pick(self.x_pair, self.first_x, i < 0, at, BRICK)
        elif inside_x:
            at = HALO * extent_x * channels + BRICK * i
            tile = self.pick(self.y_pair, self.first_y, j < 0, at, BRICK)
        else:
            at = 2 * HALO * HALO * channels + BRICK * int(i > 0)
            tile = self.pick(self.corner_pair, self.first_y, j < 0, at, BRICK)
        return tile


class Sums:
    def __init__(self, sums, squares):
        self.sums, self.squares = sums, squares

    def add(self, value):
        value = value.astype(F32)
        self.sums = self.sums + value
        self.squares = self.squares + value * value


def ring_groups(extent_x, extent_y):
    far = (extent_x - 1, extent_y - 1)
    groups = [(x, y) for x in range(-1, extent_x, 2) for y in range(-1, extent_y, 2)]
    corners = [g for g in groups if g[0] in (-1, far[0]) and g[1] in (-1, far[1])]
    return [g for g in groups if g not in corners], corners


def first_kernel(dims, own, masks, x_even, x_odd, y_even, y_odd, band, first_out, partial):
    channels, extent_x, extent_y, depth, _, _ = dims
    edges = Edges(dims, own, masks, (x_even, x_odd), (y_even, y_odd))
    found = {}
    zero = jnp.zeros((channels, depth), F32)
    sums = Sums(zero, zero)

    def emit(x, y, value):
        brick = (x // BRICK, y // BRICK)
        if brick not in found:
            found[brick] = edges.mask(*brick)[:1]
        value = (value() * found[brick]).astype(BF16)
        first_out[x + 1, y + 1] = value
        if 0 <= x < extent_x and 0 <= y < extent_y:
            sums.add(value)

    groups = ring_groups(extent_x, extent_y)[0]
    convolve_groups(groups, edges.column, band, channels, depth, emit)
    partial[0] = sums.sums
    partial[1] = sums.squares


def finish_kernel(dims, own, masks, *refs):
    x_even, x_odd, y_even, y_odd, c_even, c_odd, band, partial, corner_out, wide_masks, stats = refs
    channels, extent_x, extent_y, depth, bx, by = dims
    edges = Edges(dims, own, masks, (x_even, x_odd), (y_even, y_odd), (c_even, c_odd))
    counts = jnp.zeros((BRICK, depth), F32)
    for i in range(-1, bx + 1):
        for j in range(-1, by + 1):
            tile = edges.mask(i, j)
            wide_masks[i + 1, j + 1] = tile
            if 0 <= i < bx and 0 <= j < by:
                counts = counts + tile * float(BRICK)
    sums = Sums(partial[0], partial[1])

    outputs = []
    groups = ring_groups(extent_x, extent_y)[1]
    convolve_groups(groups, edges.column, band, channels, depth, lambda *it: outputs.append(it))

    def put(x, y, value):
        value = (value() * edges.mask(x // BRICK, y // BRICK)[:1]).astype(BF16)
        side_x, side_y = int(x >= extent_x - 1), int(y >= extent_y - 1)
        i = x - (extent_x - 1 if side_x else -1)
        j = y - (extent_y - 1 if side_y else -1)
        corner_out[2 * side_x + i, 2 * side_y + j] = value
        return value

    def is_own(x, y):
        return 0 <= x < extent_x and 0 <= y < extent_y

    for x, y, value in outputs:
        if is_own(x, y):
            sums.add(put(x, y, value))
    send_stats(stats, channels, sums.sums, sums.squares, counts)
    for x, y, value in outputs:
        if not is_own(x, y):
            put(x, y, value)


def second_kernel(dims, *refs):
    first_out, corner_out, wide_masks, received, params, band, second_out, stats, field = refs
    channels, extent_x, extent_y, depth, bx, by = dims
    scale, offset = affine(received, params[0], params[1], channels)
    edge_x, edge_y = (0, 1, extent_x, extent_x + 1), (0, 1, extent_y, extent_y + 1)
    done = set()

    def activate(x, y):
        if (x, y) in done:
            return
        done.add((x, y))
        if x + 1 in edge_x and y + 1 in edge_y:
            part = corner_out[edge_x.index(x + 1), edge_y.index(y + 1)]
        else:
            part = first_out[x + 1, y + 1]
        mask = wide_masks[x // BRICK + 1, y // BRICK + 1][:1]
        part = jnp.maximum(part.astype(F32) * scale + offset, 0.0) * mask
        field[x + 1, y + 1] = part.astype(BF16)

    zero = jnp.zeros((channels, depth), F32)
    sums = Sums(zero, zero)

    def emit(x, y, value):
        value = (value() * wide_masks[x // BRICK + 1, y // BRICK + 1][:1]).astype(BF16)
        second_out[x, y] = value
        sums.add(value)

    groups = [(x, y) for x in range(0, extent_x, 2) for y in range(0, extent_y, 2)]
    convolve_groups(
        groups, lambda x, y: field[x + 1, y + 1], band, channels, depth, emit, activate
    )
    counts = jnp.zeros((BRICK, depth), F32)
    for i in range(bx):
        for j in range(by):
            counts = counts + wide_masks[1 + i, 1 + j] * float(BRICK)
    send_stats(stats, channels, sums.sums, sums.squares, counts)


def last_kernel(dims, second_out, wide_masks, received, params, own, result, turned, ready, sent):
    channels, extent_x, _, depth, _, by = dims
    scale, offset = affine(received, params[2], params[3], channels)
    copies = []
    for start in range(0, channels, PART):
        rows = slice(start, start + PART)
        for x in range(extent_x):
            for j in range(by):
                mask = wide_masks[x // BRICK + 1, j + 1][:1]
                for y in range(BRICK):
                    at = j * BRICK + y
                    part = second_out[x, at, rows].astype(F32) * scale[rows] + offset[rows]
                    part = jnp.maximum(part + own[x, at, rows].astype(F32), 0.0) * mask
                    turned[x % 2, pl.ds(y, PART, stride=BRICK), :] = part
                ready[rows, x, j * BRICK : (j + 1) * BRICK, :] = (
                    turned[x % 2, : PART * BRICK].reshape(PART, BRICK, depth).astype(BF16)
                )
        copy = pltpu.make_async_copy(ready.at[rows], result.at[rows], sent.at[start // PART])
        copy.start()
        copies.append(copy)
    for copy in copies:
        copy.wait()


def per_device(
    features,
    brick_mask,
    conv_first,
    conv_second,
    gain_first,
    shift_first,
    gain_second,
    shift_second,
):
    channels, extent_x, extent_y, depth = features.shape
    bx, by, bz = brick_mask.shape
    dims = (channels, extent_x, extent_y, depth, bx, by)
    devices = lax.axis_size(AXES)
    shape = jax.ShapeDtypeStruct

    x_rows = HALO * extent_y * channels + BRICK * by
    y_rows = HALO * extent_x * channels + BRICK * bx
    c_rows = 2 * HALO * HALO * channels + 2 * BRICK
    turned = pltpu.VMEM((2, channels * BRICK, depth), F32)
    masks, x_even, x_odd = call(
        functools.partial(edge_kernel, dims),
        (
            shape((bx * by, BRICK, depth), F32),
            shape((x_rows, depth), BF16),
            shape((x_rows, depth), BF16),
        ),
        (
            pltpu.with_memory_space_constraint(features, pltpu.HBM),
            pltpu.with_memory_space_constraint(brick_mask.reshape(bx * by, bz), pltpu.HBM),
        ),
        scratch=[
            pltpu.VMEM((2, channels, HALO, extent_y, depth), BF16),
            pltpu.VMEM((bx * by, bz), jnp.int32),
            turned,
            pltpu.VMEM((2, HALO * extent_y * channels, depth), BF16),
            pltpu.SemaphoreType.DMA((2,)),
            pltpu.SemaphoreType.DMA,
        ],
        far=(0, 1),
    )
    x_pair = swap(x_even, x_odd, "region")
    own, y_even, y_odd = call(
        functools.partial(gather_kernel, dims),
        (
            shape((extent_x, extent_y, channels, depth), BF16),
            shape((y_rows, depth), BF16),
            shape((y_rows, depth), BF16),
        ),
        (features, masks),
        scratch=[turned],
    )
    y_pair = swap(y_even, y_odd, "strip")
    corners = call(
        functools.partial(corner_kernel, dims),
        (shape((c_rows, depth), BF16), shape((c_rows, depth), BF16)),
        x_pair,
    )
    c_pair = swap(*corners, "strip")

    band_shape = shape((12 * channels, 16 * channels), BF16)
    first_band, second_band, params = call(
        prepare_kernel,
        (band_shape, band_shape, shape((4, channels, depth), F32)),
        (
            conv_first,
            conv_second,
            jnp.stack([gain_first, shift_first, gain_second, shift_second]),
        ),
    )
    wide_shape = (extent_x + 2, extent_y + 2, channels, depth)
    first_out, partial = call(
        functools.partial(first_kernel, dims),
        (shape(wide_shape, BF16), shape((2, channels, depth), F32)),
        (own, masks, *x_pair, *y_pair, first_band),
    )
    corner_out, wide_masks, sent = call(
        functools.partial(finish_kernel, dims),
        (
            shape((4, 4, channels, depth), BF16),
            shape((bx + 2, by + 2, BRICK, depth), F32),
            shape((devices, 128), F32),
        ),
        (own, masks, *x_pair, *y_pair, *c_pair, first_band, partial),
    )
    received = lax.all_to_all(sent, AXES, 0, 0, tiled=True)
    second_out, sent = call(
        functools.partial(second_kernel, dims),
        (
            shape((extent_x, extent_y, channels, depth), BF16),
            shape((devices, 128), F32),
        ),
        (first_out, corner_out, wide_masks, received, params, second_band),
        scratch=[pltpu.VMEM(wide_shape, BF16)],
    )
    received = lax.all_to_all(sent, AXES, 0, 0, tiled=True)
    return call(
        functools.partial(last_kernel, dims),
        shape(features.shape, BF16),
        (second_out, wide_masks, received, params, own),
        scratch=[
            turned,
            pltpu.VMEM(features.shape, BF16),
            pltpu.SemaphoreType.DMA((channels // PART,)),
        ],
        far_out=True,
    )


def solution(mesh):
    in_specs = (
        P(None, "region", "strip", None),
        P("region", "strip", None),
        P(),
        P(),
        P(),
        P(),
        P(),
        P(),
    )
    out_specs = P(None, "region", "strip", None)
    return jax.shard_map(
        per_device, mesh=mesh, in_specs=in_specs, out_specs=out_specs, check_vma=False
    )
```
